32 devices in a mesh: ctx: 4 (over y, x), tp: 8 (over z, core).
Axes of the slice: x: 2, y: 2, z: 4, core: 2. Of those that a mesh axis runs over, the one named last changes fastest.
Arguments:
- query_proj: bfloat16 [1536, 4096], P('ctx', 'tp'), may hold values from -16 to 16
- key_proj: bfloat16 [1536, 4096], P('ctx', 'tp'), may hold values from -16 to 16
- value_proj: bfloat16 [1536, 4096], P('ctx', 'tp'), may hold values from -6 to 6
- query_gain: float32 [4096], P('tp'), may hold values from 0.1 to 1.9
- key_gain: float32 [4096], P('tp'), may hold values from 0.1 to 1.9
- stripe_of: int32 [8], replicated, may hold values from 0 to 7, as said below
- grad_out: bfloat16 [1536, 4096], P('ctx', 'tp'), may hold values from -6 to 6
Outputs:
- grad_query: bfloat16 [1536, 4096], P('ctx', 'tp')
- grad_key: bfloat16 [1536, 4096], P('ctx', 'tp')
- grad_value: bfloat16 [1536, 4096], P('ctx', 'tp')
- grad_query_gain: float32 [4096], P('tp')
- grad_key_gain: float32 [4096], P('tp')
The draws below stay inside these ranges and needn't reach their ends.
Inputs may be any that keep to these rules, and one draw needn't show every extreme that they name: `stripe_of`: each number of 0 to 7 appears once, and entries 2 d and 2 d + 1 sum to 7 for every d.
All inputs are finite; a program needn't handle non-finite values.
Results may differ from the reference program's by a relative error of at most 0.012.
The reference program's roundings to bfloat16 on the way count: a program that leaves them out, or rounds other values in their place, can miss the bound.
Values may be sent and summed in bfloat16 or wider, within the bound.
No kernel may reach another device: no remote copies, remote signals or barrier semaphores. Data moves between devices by JAX's collectives and lax.ppermute only.
A program may use at most 128 MiB of HBM per device.

```python
import jax
import jax.numpy as jnp
from jax import lax

H = 32
HD = 128
D = 4096
TOK_DEV = 384
SEQ = 1536
STRIPE = 192


def stripe_table(base_key):
    group_count = SEQ // TOK_DEV
    table_key = jax.random.fold_in(base_key, 7)
    order_list = jax.random.permutation(jax.random.fold_in(table_key, 1), group_count)
    flip_bits = jax.random.randint(jax.random.fold_in(table_key, 2), (group_count,), 0, 2)
    first_stripe = jnp.where(flip_bits == 1, 2 * group_count - 1 - order_list, order_list)
    second_stripe = 2 * group_count - 1 - first_stripe
    return jnp.stack([first_stripe, second_stripe], axis=1).reshape(2 * group_count).astype(jnp.int32)


def shaped_field(base_key, salt_value):
    rough_field = jnp.clip(jax.random.normal(jax.random.fold_in(base_key, salt_value), (SEQ, D), jnp.float32), -5.0, 5.0)
    return rough_field


def draw_query_proj(key, part):
    return shaped_field(key, 101).astype(jnp.bfloat16)


def draw_key_proj(key, part):
    return shaped_field(key, 201).astype(jnp.bfloat16)


def draw_stripe_of(key, part):
    return stripe_table(key)


def block_levels(rng, shape, pieces, least, largest):
    def one(dim, blocks):
        heights = jax.random.uniform(jax.random.fold_in(jax.random.fold_in(rng, 6), dim), (blocks,), jnp.float32, least / len(pieces), largest / len(pieces))
        return jnp.repeat(jnp.exp(heights), shape[dim] // blocks).reshape((-1,) + (1,) * (len(shape) - dim - 1))

    factor_of = one(*pieces[0])
    for cut in pieces[1:]:
        factor_of = factor_of * one(*cut)
    return factor_of


def centred(stream_key, shape, spread, most, split=(), kind=jnp.bfloat16):
    array = spread * jax.random.normal(stream_key, shape, jnp.float32)
    if split:
        array = array * block_levels(stream_key, shape, split, -0.22, 0.18)
    return jnp.clip(array, -most, most).astype(kind)


def setup_inputs(seed: int = 0) -> dict:
    streams_of = jax.random.split(jax.random.key(seed), 8)
    query_proj = draw_query_proj(jax.random.fold_in(streams_of[7], 71), 0)
    key_proj = draw_key_proj(jax.random.fold_in(streams_of[7], 71), 0)
    value_proj = centred(streams_of[2], (SEQ, D), 1.0, 6.0, ((0, 4), (1, 8)))
    query_gain = jnp.clip(1.0 + 0.18 * jax.random.normal(streams_of[3], (D,), jnp.float32), 0.1, 1.9)
    key_gain = jnp.clip(1.0 + 0.18 * jax.random.normal(streams_of[4], (D,), jnp.float32), 0.1, 1.9)
    stripe_of = draw_stripe_of(jax.random.fold_in(streams_of[7], 71), 0)
    grad_out = centred(streams_of[6], (SEQ, D), 1.0, 6.0, ((0, 4), (1, 8)))
    return dict(query_proj=query_proj, key_proj=key_proj, value_proj=value_proj, query_gain=query_gain, key_gain=key_gain, stripe_of=stripe_of, grad_out=grad_out)


EPSILON = 1e-06

def normalize(raw_rows, gain_row):
    float_rows = raw_rows.astype(jnp.float32)
    inverse_norm = lax.rsqrt(lax.optimization_barrier(jnp.sum(float_rows * float_rows, axis=1, keepdims=True)) / D + EPSILON)
    unit_rows = float_rows * inverse_norm
    return (inverse_norm, unit_rows, (unit_rows * gain_row).astype(jnp.bfloat16))

def split_heads(matrix):
    return matrix.reshape(SEQ, H, HD).transpose(1, 0, 2)

def merge_heads(stacked):
    return stacked.transpose(1, 0, 2).reshape(SEQ, H * HD)

def finish_norm(inverse_norm, unit_rows, normed_grad, gain_row):
    unit_grad = normed_grad * gain_row
    centered = unit_grad - unit_rows * lax.optimization_barrier(jnp.mean(unit_grad * unit_rows, axis=1, keepdims=True))
    return (inverse_norm * centered).astype(jnp.bfloat16)

def reference(query_proj, key_proj, value_proj, query_gain, key_gain, stripe_of, grad_out):
    query_inverse, query_unit, query_normed = normalize(query_proj, query_gain)
    key_inverse, key_unit, key_normed = normalize(key_proj, key_gain)
    storage_rows = jnp.arange(SEQ, dtype=jnp.int32)
    positions = stripe_of[storage_rows // STRIPE] * STRIPE + storage_rows % STRIPE
    allowed = positions[None, :] <= positions[:, None]
    inverse_root = HD ** (-0.5)

    def one_head(operands):
        query_head, key_head, value_head, grad_head = operands
        scores = jnp.dot(query_head, key_head.T, preferred_element_type=jnp.float32) * inverse_root
        scores = jnp.where(allowed, scores, -jnp.inf)
        row_best = lax.optimization_barrier(jnp.max(scores, axis=1, keepdims=True))
        exponent = jnp.exp(scores - row_best)
        row_total = lax.optimization_barrier(jnp.sum(exponent, axis=1, keepdims=True))
        log_total = row_best + jnp.log(row_total)
        grad_probs = jnp.dot(grad_head, value_head.T, preferred_element_type=jnp.float32)
        probs = jnp.exp(scores - log_total)
        row_delta = lax.optimization_barrier(jnp.sum(probs * grad_probs, axis=1, keepdims=True))
        grad_scores = probs * (grad_probs - row_delta)
        probs_rounded = probs.astype(jnp.bfloat16)
        scores_rounded = grad_scores.astype(jnp.bfloat16)
        value_grad = jnp.dot(probs_rounded.T, grad_head, preferred_element_type=jnp.float32)
        query_grad = jnp.dot(scores_rounded, key_head, preferred_element_type=jnp.float32) * inverse_root
        key_grad = jnp.dot(scores_rounded.T, query_head, preferred_element_type=jnp.float32) * inverse_root
        return (query_grad, key_grad, value_grad)
    query_grads, key_grads, value_grads = lax.map(one_head, (split_heads(query_normed), split_heads(key_normed), split_heads(value_proj), split_heads(grad_out)))
    query_normed_grad = merge_heads(query_grads)
    key_normed_grad = merge_heads(key_grads)
    grad_value = merge_heads(value_grads).astype(jnp.bfloat16)
    grad_query_gain = lax.optimization_barrier(jnp.sum(query_normed_grad * query_unit, axis=0))
    grad_key_gain = lax.optimization_barrier(jnp.sum(key_normed_grad * key_unit, axis=0))
    grad_query = finish_norm(query_inverse, query_unit, query_normed_grad, query_gain)
    grad_key = finish_norm(key_inverse, key_unit, key_normed_grad, key_gain)
    return (grad_query, grad_key, grad_value, grad_query_gain, grad_key_gain)
```

```python
import functools
import math

import jax
import jax.numpy as jnp
from jax import lax
from jax.experimental import pallas as pl
from jax.experimental.pallas import tpu as pltpu
from jax.sharding import PartitionSpec as P

HD = 128
EPSILON = 1e-06
VMEM = pl.BlockSpec(memory_space=pltpu.VMEM)
SMEM = pl.BlockSpec(memory_space=pltpu.SMEM)
ROWS_BY_ROWS = (((1,), (1,)), ((), ()))
COLUMNS_BY_COLUMNS = (((0,), (0,)), ((), ()))


def head_columns(head):
    return pl.ds(pl.multiple_of(head * HD, HD), HD)


def down_rows(row_vector):
    return jnp.broadcast_to(row_vector, (HD, row_vector.shape[1])).T


def lane_folded(squares):
    total = squares[:, :HD]
    for start in range(HD, squares.shape[1], HD):
        total = total + squares[:, start : start + HD]
    return total


def cut_kernel(peers, query_ref, key_ref, value_ref, grad_ref, *out_refs):
    device = lax.axis_index("ctx")
    for mask in range(peers):
        columns = head_columns(device ^ mask)
        out_refs[mask][0] = value_ref[:, columns]
        out_refs[mask][1] = grad_ref[:, columns]
    for row, ref in enumerate((query_ref, key_ref)):
        rows = ref[...].astype(jnp.float32)
        folded = lane_folded(rows * rows)
        out_refs[peers][row : row + 1, :] = jnp.sum(folded.T, axis=0, keepdims=True)


def normalize_kernel(peers, width, squares_ref, query_ref, key_ref, query_gain_ref, key_gain_ref, *out_refs):
    device = lax.axis_index("ctx")
    inverse = lax.rsqrt(squares_ref[...] / width + EPSILON)
    sides = ((query_ref, query_gain_ref), (key_ref, key_gain_ref))
    for side, (ref, gain_ref) in enumerate(sides):
        scale = down_rows(inverse[side : side + 1, :])
        for mask in range(peers):
            columns = head_columns(device ^ mask)
            unit = ref[:, columns].astype(jnp.float32) * scale
            out_refs[mask][side] = (unit * gain_ref[:, columns]).astype(jnp.bfloat16)


def attend_kernel(peers, block, stripe_ref, *refs):
    normed_refs, plain_refs = refs[:peers], refs[peers : 2 * peers]
    grads_refs, sums_refs = refs[2 * peers : 3 * peers], refs[3 * peers : 4 * peers]
    query, key, value, grad, query_grad, key_grad, value_grad, scores, grad_probs = refs[4 * peers :]
    device = lax.axis_index("ctx")
    rows = query.shape[0]
    token_count = rows // peers
    stripe = token_count // 2
    places = []
    for mask in range(peers):
        for slot in range(2):
            number = stripe_ref[2 * (device ^ mask) + slot]
            places.append((mask, slot, pl.ds(pl.multiple_of(number * stripe, stripe), stripe)))
    for mask, slot, place in places:
        local = slice(slot * stripe, (slot + 1) * stripe)
        query[place, :] = normed_refs[mask][0, local, :]
        key[place, :] = normed_refs[mask][1, local, :]
        value[place, :] = plain_refs[mask][0, local, :]
        grad[place, :] = plain_refs[mask][1, local, :]
    inverse_root = HD ** (-0.5)
    exponent_scale = inverse_root * math.log2(math.e)
    count = rows // block
    visible = lax.broadcasted_iota(jnp.int32, (block, block), 0) <= lax.broadcasted_iota(
        jnp.int32, (block, block), 1
    )
    for index in range(count):
        here = slice(index * block, (index + 1) * block)
        query_block, grad_block = query[here, :], grad[here, :]
        best = None
        for other in range(index + 1):
            there = slice(other * block, (other + 1) * block)
            tile = lax.dot_general(
                key[there, :], query_block, ROWS_BY_ROWS, preferred_element_type=jnp.float32
            )
            if other == index:
                tile = jnp.where(visible, tile, -jnp.inf)
            scores[there, :] = tile
            tile_best = jnp.max(tile, axis=0, keepdims=True)
            best = tile_best if best is None else jnp.maximum(best, tile_best)
        total = delta = None
        for other in range(index + 1):
            there = slice(other * block, (other + 1) * block)
            probs = jnp.exp2((scores[there, :] - best) * exponent_scale)
            tile = lax.dot_general(
                value[there, :], grad_block, ROWS_BY_ROWS, preferred_element_type=jnp.float32
            )
            scores[there, :] = probs
            grad_probs[there, :] = tile
            tile_total = jnp.sum(probs, axis=0, keepdims=True)
            tile_delta = jnp.sum(probs * tile, axis=0, keepdims=True)
            total = tile_total if total is None else total + tile_total
            delta = tile_delta if delta is None else delta + tile_delta
        inverse_total = 1.0 / total
        delta = delta * inverse_total
        query_sum = None
        for other in range(index + 1):
            there = slice(other * block, (other + 1) * block)
            probs = scores[there, :] * inverse_total
            scores_rounded = (probs * (grad_probs[there, :] - delta)).astype(jnp.bfloat16)
            value_part = jnp.dot(
                probs.astype(jnp.bfloat16), grad_block, preferred_element_type=jnp.float32
            )
            key_part = jnp.dot(scores_rounded, query_block, preferred_element_type=jnp.float32)
            query_part = lax.dot_general(
                scores_rounded, key[there, :], COLUMNS_BY_COLUMNS, preferred_element_type=jnp.float32
            )
            if other == index:
                value_grad[there, :] = value_part
                key_grad[there, :] = key_part
            else:
                value_grad[there, :] += value_part
                key_grad[there, :] += key_part
            query_sum = query_part if query_sum is None else query_sum + query_part
        query_grad[here, :] = query_sum
    gain_sums = [None, None]
    for mask, slot, place in places:
        local = slice(slot * stripe, (slot + 1) * stripe)
        for side, (grad_rows, normed) in enumerate(((query_grad, query), (key_grad, key))):
            normed_grad = grad_rows[place, :] * inverse_root
            grads_refs[mask][side, local, :] = normed_grad.astype(jnp.bfloat16)
            terms = normed_grad * normed[place, :].astype(jnp.float32)
            row = 2 * side + slot
            sums_refs[mask][row : row + 1, :] = jnp.sum(terms.T, axis=0, keepdims=True)
            part = jnp.sum(terms, axis=0, keepdims=True)
            gain_sums[side] = part if gain_sums[side] is None else gain_sums[side] + part
        grads_refs[mask][2, local, :] = value_grad[place, :].astype(jnp.bfloat16)
    for mask in range(peers):
        for side in range(2):
            sums_refs[mask][4 + side : 5 + side, :HD] = gain_sums[side]


def finish_kernel(peers, width, squares_ref, means_ref, query_ref, key_ref, query_gain_ref, key_gain_ref, *refs):
    grads_refs, sums_refs = refs[:peers], refs[peers : 2 * peers]
    grad_query, grad_key, grad_value, query_gain_grad, key_gain_grad = refs[2 * peers :]
    device = lax.axis_index("ctx")
    stripe = means_ref.shape[1]
    inverse = lax.rsqrt(squares_ref[...] / width + EPSILON)
    sides = (
        (query_ref, query_gain_ref, grad_query, query_gain_grad),
        (key_ref, key_gain_ref, grad_key, key_gain_grad),
    )
    for side, (ref, gain_ref, out_ref, gain_out_ref) in enumerate(sides):
        scale = down_rows(inverse[side : side + 1, :])
        for slot in range(2):
            local = slice(slot * stripe, (slot + 1) * stripe)
            row = 2 * side + slot
            mean = down_rows(means_ref[row : row + 1, :] / width)
            for mask in range(peers):
                columns = head_columns(device ^ mask)
                unit = ref[local, columns].astype(jnp.float32) * scale[local]
                unit_grad = grads_refs[mask][side, local, :].astype(jnp.float32) * gain_ref[:, columns]
                out_ref[local, columns] = (scale[local] * (unit_grad - unit * mean)).astype(jnp.bfloat16)
        for mask in range(peers):
            columns = head_columns(device ^ mask)
            gain_out_ref[:, columns] = sums_refs[mask][4 + side : 5 + side, :HD] / gain_ref[:, columns]
    for mask in range(peers):
        grad_value[:, head_columns(device ^ mask)] = grads_refs[mask][2]


def swap(array, axis, size, mask):
    return lax.ppermute(array, axis, [(index, index ^ mask) for index in range(size)])


def sum_over(array, axis, size):
    mask = 1
    while mask < size:
        array = array + swap(array, axis, size, mask)
        mask *= 2
    return array


def call(kernel, name, out_shape, operands, in_specs=None, scratch_shapes=()):
    return pl.pallas_call(
        kernel,
        name=name,
        out_shape=out_shape,
        in_specs=in_specs or [VMEM] * len(operands),
        out_specs=[VMEM] * len(out_shape),
        scratch_shapes=scratch_shapes,
    )(*operands)


def whole_heads(peers, tp_size, query_proj, key_proj, value_proj, query_gain, key_gain, stripe_of, grad_out):
    token_count, local_width = query_proj.shape
    width = local_width * tp_size
    rows = token_count * peers
    stripe = token_count // 2
    shape = jax.ShapeDtypeStruct
    query_gain_row, key_gain_row = query_gain[None], key_gain[None]
    pair = shape((2, token_count, HD), jnp.bfloat16)
    *plain, squares = call(
        functools.partial(cut_kernel, peers),
        "cut",
        [pair] * peers + [shape((2, token_count), jnp.float32)],
        (query_proj, key_proj, value_proj, grad_out),
    )
    plain = [plain[0]] + [swap(plain[mask], "ctx", peers, mask) for mask in range(1, peers)]
    squares = sum_over(squares, "tp", tp_size)
    normed = call(
        functools.partial(normalize_kernel, peers, width),
        "normalize",
        [pair] * peers,
        (squares, query_proj, key_proj, query_gain_row, key_gain_row),
    )
    normed = [normed[0]] + [swap(normed[mask], "ctx", peers, mask) for mask in range(1, peers)]
    block = math.gcd(rows, 256)
    row_block = lambda dtype: pltpu.VMEM((rows, HD), dtype)
    outs = call(
        functools.partial(attend_kernel, peers, block),
        "attend",
        [shape((3, token_count, HD), jnp.bfloat16)] * peers + [shape((8, stripe), jnp.float32)] * peers,
        (stripe_of, *normed, *plain),
        in_specs=[SMEM] + [VMEM] * (2 * peers),
        scratch_shapes=[row_block(jnp.bfloat16)] * 4
        + [row_block(jnp.float32)] * 3
        + [pltpu.VMEM((rows, block), jnp.float32)] * 2,
    )
    grads, sums = outs[:peers], outs[peers:]
    sums = [sums[0]] + [swap(sums[mask], "ctx", peers, mask) for mask in range(1, peers)]
    grads = [grads[0]] + [swap(grads[mask], "ctx", peers, mask) for mask in range(1, peers)]
    means = sum_over(functools.reduce(jnp.add, [part[:4] for part in sums]), "tp", tp_size)
    whole = shape((token_count, local_width), jnp.bfloat16)
    row = shape((1, local_width), jnp.float32)
    grad_query, grad_key, grad_value, query_gain_grad, key_gain_grad = call(
        functools.partial(finish_kernel, peers, width),
        "finish",
        [whole] * 3 + [row] * 2,
        (squares, means, query_proj, key_proj, query_gain_row, key_gain_row, *grads, *sums),
    )
    return (grad_query, grad_key, grad_value, query_gain_grad[0], key_gain_grad[0])


def row_positions(stripe_list, offset, count, stripe):
    storage_rows = offset + lax.iota(jnp.int32, count)
    stripe_ids = lax.iota(jnp.int32, stripe_list.shape[0])
    matches = (storage_rows // stripe)[:, None] == stripe_ids[None, :]
    chosen = jnp.sum(jnp.where(matches, stripe_list[None, :], 0), axis=1)
    return chosen * stripe + storage_rows % stripe


def block_scores(query_heads, grad_heads, query_places, key_heads, value_heads, key_places):
    scores = jnp.einsum(
        "thd,khd->htk", query_heads, key_heads, preferred_element_type=jnp.float32
    ) * HD ** (-0.5)
    visible = key_places[None, :] <= query_places[:, None]
    scores = jnp.where(visible[None], scores, -jnp.inf)
    grad_probs = jnp.einsum(
        "thd,khd->htk", grad_heads, value_heads, preferred_element_type=jnp.float32
    )
    return (scores, grad_probs)


def block_weights(scores, grad_probs, log_total, row_delta):
    probs = jnp.exp(scores - log_total[:, :, None])
    grad_scores = probs * (grad_probs - row_delta[:, :, None])
    return (probs.astype(jnp.bfloat16), grad_scores.astype(jnp.bfloat16))


def finish_norm(inverse_norm, unit_rows, unit_grad, mean_rows):
    return (inverse_norm * (unit_grad - unit_rows * mean_rows[:, None])).astype(jnp.bfloat16)


def gathered_blocks(tp_size, query_proj, key_proj, value_proj, query_gain, key_gain, stripe_of, grad_out):
    token_count, local_width = query_proj.shape
    local_heads = local_width // HD
    width = local_width * tp_size
    stripe = token_count // 2
    device = lax.axis_index("ctx")
    query_rows = query_proj.astype(jnp.float32)
    key_rows = key_proj.astype(jnp.float32)
    query_square, key_square = lax.psum(
        (jnp.sum(query_rows * query_rows, axis=1), jnp.sum(key_rows * key_rows, axis=1)), "tp"
    )
    query_inverse = lax.rsqrt(query_square / width + EPSILON)[:, None]
    key_inverse = lax.rsqrt(key_square / width + EPSILON)[:, None]
    query_unit = query_rows * query_inverse
    key_unit = key_rows * key_inverse
    query_normed = (query_unit * query_gain).astype(jnp.bfloat16)
    key_normed = (key_unit * key_gain).astype(jnp.bfloat16)
    query_places = row_positions(stripe_of, device * token_count, token_count, stripe)
    query_heads = query_normed.reshape(token_count, local_heads, HD)
    grad_heads = grad_out.reshape(token_count, local_heads, HD)
    key_heads = key_normed.reshape(token_count, local_heads, HD)
    value_heads = value_proj.reshape(token_count, local_heads, HD)
    start_best = jnp.full((local_heads, token_count), -1e30, jnp.float32)
    zero_rows = jnp.zeros((local_heads, token_count), jnp.float32)
    key_piece = lax.all_gather(key_normed, "ctx", axis=0, tiled=True)
    value_piece = lax.all_gather(value_proj, "ctx", axis=0, tiled=True)
    row_count = key_piece.shape[0]
    block = math.gcd(row_count, 512)
    key_blocks = key_piece.reshape(row_count // block, block, local_heads, HD)
    value_blocks = value_piece.reshape(row_count // block, block, local_heads, HD)

    def forward_advance(status, entry):
        row_best, row_total, weighted = status
        key_block, value_block, block_index = entry
        key_places = row_positions(stripe_of, block_index * block, block, stripe)
        scores, grad_probs = block_scores(
            query_heads, grad_heads, query_places, key_block, value_block, key_places
        )
        new_best = jnp.maximum(row_best, jnp.max(scores, axis=2))
        decay_factor = jnp.exp(row_best - new_best)
        exponent = jnp.exp(scores - new_best[:, :, None])
        return (
            (
                new_best,
                row_total * decay_factor + jnp.sum(exponent, axis=2),
                weighted * decay_factor + jnp.sum(exponent * grad_probs, axis=2),
            ),
            None,
        )

    block_ids = jnp.arange(row_count // block, dtype=jnp.int32)
    row_best, row_total, weighted = lax.scan(
        forward_advance, (start_best, zero_rows, zero_rows), (key_blocks, value_blocks, block_ids)
    )[0]
    log_total = row_best + jnp.log(row_total)
    row_delta = weighted / row_total
    zero_grads = jnp.zeros((token_count, local_heads, HD), jnp.float32)
    total_all, delta_all = (
        lax.all_gather(log_total, "ctx", axis=1, tiled=True),
        lax.all_gather(row_delta, "ctx", axis=1, tiled=True),
    )

    def query_fold(carry_state, pieces):
        query_piece, grad_piece = pieces
        row_count = query_piece.shape[0]
        block = math.gcd(row_count, 512)
        query_blocks = query_piece.reshape(row_count // block, block, local_heads, HD)
        grad_blocks = grad_piece.reshape(row_count // block, block, local_heads, HD)

        def query_advance(status, entry):
            key_grad, value_grad = status
            query_block, grad_block, block_index = entry
            first_row = block_index * block
            block_places = row_positions(stripe_of, first_row, block, stripe)
            block_total = lax.dynamic_slice_in_dim(total_all, first_row, block, 1)
            block_delta = lax.dynamic_slice_in_dim(delta_all, first_row, block, 1)
            scores, grad_probs = block_scores(
                query_block, grad_block, block_places, key_heads, value_heads, query_places
            )
            probs_rounded, scores_rounded = block_weights(
                scores, grad_probs, block_total, block_delta
            )
            value_grad = value_grad + jnp.einsum(
                "htk,thd->khd", probs_rounded, grad_block, preferred_element_type=jnp.float32
            )
            key_grad = key_grad + jnp.einsum(
                "htk,thd->khd", scores_rounded, query_block, preferred_element_type=jnp.float32
            )
            return ((key_grad, value_grad), None)

        block_ids = jnp.arange(row_count // block, dtype=jnp.int32)
        return lax.scan(query_advance, carry_state, (query_blocks, grad_blocks, block_ids))[0]

    key_grad, value_grad = query_fold(
        (zero_grads, zero_grads),
        (
            lax.all_gather(query_normed, "ctx", axis=0, tiled=True),
            lax.all_gather(grad_out, "ctx", axis=0, tiled=True),
        ),
    )

    def key_fold(carry_state, pieces):
        key_piece, value_piece = pieces
        row_count = key_piece.shape[0]
        block = math.gcd(row_count, 512)
        key_blocks = key_piece.reshape(row_count // block, block, local_heads, HD)
        value_blocks = value_piece.reshape(row_count // block, block, local_heads, HD)

        def key_advance(query_grad, entry):
            key_block, value_block, block_index = entry
            key_places = row_positions(stripe_of, block_index * block, block, stripe)
            scores, grad_probs = block_scores(
                query_heads, grad_heads, query_places, key_block, value_block, key_places
            )
            probs_rounded, scores_rounded = block_weights(scores, grad_probs, log_total, row_delta)
            query_grad = query_grad + jnp.einsum(
                "htk,khd->thd", scores_rounded, key_block, preferred_element_type=jnp.float32
            )
            return (query_grad, None)

        block_ids = jnp.arange(row_count // block, dtype=jnp.int32)
        return lax.scan(key_advance, carry_state, (key_blocks, value_blocks, block_ids))[0]

    query_grad = key_fold(
        zero_grads,
        (
            lax.all_gather(key_normed, "ctx", axis=0, tiled=True),
            lax.all_gather(value_proj, "ctx", axis=0, tiled=True),
        ),
    )
    inverse_root = HD ** (-0.5)
    query_normed_grad = (query_grad * inverse_root).reshape(token_count, local_width)
    key_normed_grad = (key_grad * inverse_root).reshape(token_count, local_width)
    grad_value = value_grad.reshape(token_count, local_width).astype(jnp.bfloat16)
    query_unit_grad = query_normed_grad * query_gain
    key_unit_grad = key_normed_grad * key_gain
    query_mean_terms, key_mean_terms = lax.psum(
        (jnp.sum(query_unit_grad * query_unit, axis=1), jnp.sum(key_unit_grad * key_unit, axis=1)),
        "tp",
    )
    grad_query = finish_norm(query_inverse, query_unit, query_unit_grad, query_mean_terms / width)
    grad_key = finish_norm(key_inverse, key_unit, key_unit_grad, key_mean_terms / width)
    grad_query_gain, grad_key_gain = lax.psum(
        (
            jnp.sum(query_normed_grad * query_unit, axis=0),
            jnp.sum(key_normed_grad * key_unit, axis=0),
        ),
        "ctx",
    )
    return (grad_query, grad_key, grad_value, grad_query_gain, grad_key_gain)


def solution(mesh):
    peers, tp_size = mesh.shape["ctx"], mesh.shape["tp"]

    def per_device(query_proj, *others):
        local_heads = query_proj.shape[1] // HD
        whole = local_heads == peers and peers & (peers - 1) == 0 and tp_size & (tp_size - 1) == 0
        plan = functools.partial(whole_heads, peers) if whole else gathered_blocks
        return plan(tp_size, query_proj, *others)

    placed = (P("ctx", "tp"), P("ctx", "tp"), P("ctx", "tp"), P("tp"), P("tp"), P(), P("ctx", "tp"))
    return jax.shard_map(
        per_device,
        mesh=mesh,
        in_specs=placed,
        out_specs=(P("ctx", "tp"), P("ctx", "tp"), P("ctx", "tp"), P("tp"), P("tp")),
        check_vma=False,
    )
```

```python
import functools
import math

import jax
import jax.numpy as jnp
from jax import lax
from jax.experimental import pallas as pl
from jax.experimental.pallas import tpu as pltpu
from jax.sharding import PartitionSpec as P

HD = 128
EPSILON = 1e-06
VMEM = pl.BlockSpec(memory_space=pltpu.VMEM)
SMEM = pl.BlockSpec(memory_space=pltpu.SMEM)
HBM = pl.BlockSpec(memory_space=pltpu.HBM)
ANY = pl.BlockSpec(memory_space=pl.ANY)
ROWS_BY_ROWS = (((1,), (1,)), ((), ()))
COLUMNS_BY_COLUMNS = (((0,), (0,)), ((), ()))


def head_columns(head):
    return pl.ds(pl.multiple_of(head * HD, HD), HD)


def down_rows(row_vector):
    return jnp.broadcast_to(row_vector, (HD, row_vector.shape[1])).T


def cut_kernel(peers, *refs):
    in_refs, out_refs, squares_ref, sems = refs[:4], refs[4 : 4 + peers], refs[4 + peers], refs[5 + peers]
    device = lax.axis_index("ctx")
    loads = []
    for index, ref in enumerate(in_refs):
        for mask in range(peers):
            load = pltpu.make_async_copy(
                ref.at[:, head_columns(device ^ mask)],
                out_refs[mask].at[index],
                sems.at[index * peers + mask],
            )
            load.start()
            loads.append(load)
    for side in range(2):
        folded = None
        for mask in range(peers):
            loads[side * peers + mask].wait()
            rows = out_refs[mask][side].astype(jnp.float32)
            folded = rows * rows if folded is None else folded + rows * rows
        squares_ref[side : side + 1, :] = jnp.sum(folded.T, axis=0, keepdims=True)
    for load in loads[2 * peers :]:
        load.wait()


def attend_kernel(peers, block, width, stripe_ref, query_gain_ref, key_gain_ref, *refs):
    raw_refs, squares_refs = refs[:peers], refs[peers : 2 * peers]
    grads_refs, sums_ref = refs[2 * peers : 3 * peers], refs[3 * peers]
    query, key, value, grad, query_grad, key_grad, value_grad, scores, grad_probs = refs[3 * peers + 1 :]
    device = lax.axis_index("ctx")
    rows = query.shape[0]
    token_count = rows // peers
    stripe = token_count // 2
    columns = head_columns(device)
    gains = (query_gain_ref[:, columns], key_gain_ref[:, columns])
    places = []
    for mask in range(peers):
        inverse = lax.rsqrt(squares_refs[mask][...] / width + EPSILON)
        scales = [down_rows(inverse[side : side + 1, :]) for side in range(2)]
        for slot in range(2):
            number = stripe_ref[2 * (device ^ mask) + slot]
            place = pl.ds(pl.multiple_of(number * stripe, stripe), stripe)
            local = slice(slot * stripe, (slot + 1) * stripe)
            places.append((mask, slot, place, local))
            for side, normed in enumerate((query, key)):
                unit = raw_refs[mask][side, local, :].astype(jnp.float32) * scales[side][local]
                normed[place, :] = (unit * gains[side]).astype(jnp.bfloat16)
            value[place, :] = raw_refs[mask][2, local, :]
            grad[place, :] = raw_refs[mask][3, local, :]
    inverse_root = HD ** (-0.5)
    exponent_scale = inverse_root * math.log2(math.e)
    count = rows // block
    visible = lax.broadcasted_iota(jnp.int32, (block, block), 0) <= lax.broadcasted_iota(
        jnp.int32, (block, block), 1
    )
    for index in range(count):
        here = slice(index * block, (index + 1) * block)
        query_block, grad_block = query[here, :], grad[here, :]
        best = None
        for other in range(index + 1):
            there = slice(other * block, (other + 1) * block)
            tile = lax.dot_general(
                key[there, :], query_block, ROWS_BY_ROWS, preferred_element_type=jnp.float32
            )
            if other == index:
                tile = jnp.where(visible, tile, -jnp.inf)
            scores[there, :] = tile
            tile_best = jnp.max(tile, axis=0, keepdims=True)
            best = tile_best if best is None else jnp.maximum(best, tile_best)
        total = delta = None
        for other in range(index + 1):
            there = slice(other * block, (other + 1) * block)
            probs = jnp.exp2((scores[there, :] - best) * exponent_scale)
            tile = lax.dot_general(
                value[there, :], grad_block, ROWS_BY_ROWS, preferred_element_type=jnp.float32
            )
            scores[there, :] = probs
            grad_probs[there, :] = tile
            tile_total = jnp.sum(probs, axis=0, keepdims=True)
            tile_delta = jnp.sum(probs * tile, axis=0, keepdims=True)
            total = tile_total if total is None else total + tile_total
            delta = tile_delta if delta is None else delta + tile_delta
        inverse_total = 1.0 / total
        delta = delta * inverse_total
        query_sum = None
        for other in range(index + 1):
            there = slice(other * block, (other + 1) * block)
            probs = scores[there, :] * inverse_total
            scores_rounded = (probs * (grad_probs[there, :] - delta)).astype(jnp.bfloat16)
            value_part = jnp.dot(
                probs.astype(jnp.bfloat16), grad_block, preferred_element_type=jnp.float32
            )
            key_part = jnp.dot(scores_rounded, query_block, preferred_element_type=jnp.float32)
            query_part = lax.dot_general(
                scores_rounded, key[there, :], COLUMNS_BY_COLUMNS, preferred_element_type=jnp.float32
            )
            if other == index:
                value_grad[there, :] = value_part
                key_grad[there, :] = key_part
            else:
                value_grad[there, :] += value_part
                key_grad[there, :] += key_part
            query_sum = query_part if query_sum is None else query_sum + query_part
        query_grad[here, :] = query_sum
    gain_sums = [None, None]
    for mask, slot, place, local in places:
        for side, (grad_rows, normed) in enumerate(((query_grad, query), (key_grad, key))):
            normed_grad = grad_rows[place, :] * inverse_root
            grads_refs[mask][side, local, :] = normed_grad.astype(jnp.bfloat16)
            terms = normed_grad * normed[place, :].astype(jnp.float32)
            row = 4 * mask + 2 * side + slot
            sums_ref[row : row + 1, :stripe] = jnp.sum(terms.T, axis=0, keepdims=True)
            part = jnp.sum(terms, axis=0, keepdims=True)
            gain_sums[side] = part if gain_sums[side] is None else gain_sums[side] + part
        grads_refs[mask][2, local, :] = value_grad[place, :].astype(jnp.bfloat16)
    first = 4 * peers
    slots = sums_ref.shape[0] - first
    mine = lax.broadcasted_iota(jnp.int32, (slots, HD), 0) == lax.axis_index("tp")
    for side in range(2):
        sums_ref[first:, side * HD : (side + 1) * HD] = jnp.where(mine, gain_sums[side], 0.0)


def finish_kernel(peers, width, squares_ref, query_gain_ref, key_gain_ref, query_ref, key_ref, *refs):
    grads_refs, sums_refs = refs[:peers], refs[peers : 2 * peers]
    out_refs, gain_out_refs = refs[2 * peers : 2 * peers + 3], refs[2 * peers + 3 : 2 * peers + 5]
    outs, out_sems = refs[2 * peers + 5 :]
    device, member = lax.axis_index("ctx"), lax.axis_index("tp")
    token_count = query_ref.shape[0]
    stripe = token_count // 2
    inverse = lax.rsqrt(squares_ref[...] / width + EPSILON)
    means = sums_refs[0][0:4, :stripe]
    for mask in range(1, peers):
        means = means + sums_refs[mask][4 * mask : 4 * mask + 4, :stripe]
    means = means / width
    scales = [down_rows(inverse[side : side + 1, :]) for side in range(2)]
    drops = [
        jnp.concatenate([down_rows(means[2 * side + slot : 2 * side + slot + 1, :]) for slot in range(2)], axis=0)
        * scales[side]
        for side in range(2)
    ]
    gain_refs, raw_refs = (query_gain_ref, key_gain_ref), (query_ref, key_ref)
    stores = []

    def store(side, mask):
        columns = head_columns(device ^ mask)
        source = grads_refs[mask].at[2] if side == 2 else outs.at[side, mask]
        copy = pltpu.make_async_copy(
            source, out_refs[side].at[:, columns], out_sems.at[side * peers + mask]
        )
        copy.start()
        stores.append(copy)

    for mask in range(peers):
        store(2, mask)
    for mask in range(peers):
        columns = head_columns(device ^ mask)
        for side in range(2):
            gain = gain_refs[side][:, columns]
            unit_grad = grads_refs[mask][side].astype(jnp.float32) * gain
            centered = unit_grad - raw_refs[side][:, columns].astype(jnp.float32) * drops[side]
            outs[side, mask] = (scales[side] * centered).astype(jnp.bfloat16)
            store(side, mask)
            slots = sums_refs[mask][4 * peers :, side * HD : (side + 1) * HD]
            mine = lax.broadcasted_iota(jnp.int32, slots.shape, 0) == member
            gain_sum = jnp.sum(jnp.where(mine, slots, 0.0), axis=0, keepdims=True)
            gain_out_refs[side][:, columns] = gain_sum / gain
    for copy in stores:
        copy.wait()


def swap(array, axis, size, mask):
    return lax.ppermute(array, axis, [(index, index ^ mask) for index in range(size)])


def sum_over_tp(array, size):
    array = array + swap(array, "tp", size, 1)
    return functools.reduce(jnp.add, [array] + [swap(array, "tp", size, mask) for mask in range(2, size, 2)])


def from_peers(array, peers):
    return [array] + [swap(array, "ctx", peers, mask) for mask in range(1, peers)]


def call(kernel, name, out_shape, operands, in_specs, out_specs, scratch_shapes, vmem_mib):
    return pl.pallas_call(
        kernel,
        name=name,
        out_shape=out_shape,
        in_specs=in_specs,
        out_specs=out_specs,
        scratch_shapes=scratch_shapes,
        compiler_params=pltpu.CompilerParams(vmem_limit_bytes=vmem_mib << 20),
    )(*operands)


def whole_heads(peers, tp_size, query_proj, key_proj, value_proj, query_gain, key_gain, stripe_of, grad_out):
    token_count, local_width = query_proj.shape
    width = local_width * tp_size
    rows = token_count * peers
    stripe = token_count // 2
    shape, semaphores = jax.ShapeDtypeStruct, pltpu.SemaphoreType.DMA
    query_gain_row, key_gain_row = query_gain[None], key_gain[None]
    *raw, squares = call(
        functools.partial(cut_kernel, peers),
        "cut",
        [shape((4, token_count, HD), jnp.bfloat16)] * peers + [shape((2, token_count), jnp.float32)],
        [pltpu.with_memory_space_constraint(array, pltpu.HBM) for array in (query_proj, key_proj, value_proj, grad_out)],
        [HBM] * 4,
        [VMEM] * (peers + 1),
        [semaphores((4 * peers,))],
        8,
    )
    raw = [raw[0]] + [swap(raw[mask], "ctx", peers, mask) for mask in range(1, peers)]
    squares = sum_over_tp(squares, tp_size)
    all_squares = from_peers(squares, peers)
    block = math.gcd(rows, 256)
    row_block = lambda dtype: pltpu.VMEM((rows, HD), dtype)
    *grads, sums = call(
        functools.partial(attend_kernel, peers, block, width),
        "attend",
        [shape((3, token_count, HD), jnp.bfloat16)] * peers
        + [shape((4 * peers + tp_size, max(stripe, 2 * HD)), jnp.float32)],
        (stripe_of, query_gain_row, key_gain_row, *raw, *all_squares),
        [SMEM] + [VMEM] * (2 + 2 * peers),
        [VMEM] * (peers + 1),
        [row_block(jnp.bfloat16)] * 4
        + [row_block(jnp.float32)] * 3
        + [pltpu.VMEM((rows, block), jnp.float32)] * 2,
        24,
    )
    grads = [grads[0]] + [swap(grads[mask], "ctx", peers, mask) for mask in range(1, peers)]
    all_sums = from_peers(sum_over_tp(sums, tp_size), peers)
    whole = shape((token_count, local_width), jnp.bfloat16)
    row = shape((1, local_width), jnp.float32)
    grad_query, grad_key, grad_value, query_gain_grad, key_gain_grad = call(
        functools.partial(finish_kernel, peers, width),
        "finish",
        [whole] * 3 + [row] * 2,
        (squares, query_gain_row, key_gain_row, query_proj, key_proj, *grads, *all_sums),
        [VMEM] * (5 + 2 * peers),
        [ANY] * 3 + [VMEM] * 2,
        [
            pltpu.VMEM((2, peers, token_count, HD), jnp.bfloat16),
            semaphores((3 * peers,)),
        ],
        8,
    )
    return (grad_query, grad_key, grad_value, query_gain_grad[0], key_gain_grad[0])


def row_positions(stripe_list, offset, count, stripe):
    storage_rows = offset + lax.iota(jnp.int32, count)
    stripe_ids = lax.iota(jnp.int32, stripe_list.shape[0])
    matches = (storage_rows // stripe)[:, None] == stripe_ids[None, :]
    chosen = jnp.sum(jnp.where(matches, stripe_list[None, :], 0), axis=1)
    return chosen * stripe + storage_rows % stripe


def block_scores(query_heads, grad_heads, query_places, key_heads, value_heads, key_places):
    scores = jnp.einsum(
        "thd,khd->htk", query_heads, key_heads, preferred_element_type=jnp.float32
    ) * HD ** (-0.5)
    visible = key_places[None, :] <= query_places[:, None]
    scores = jnp.where(visible[None], scores, -jnp.inf)
    grad_probs = jnp.einsum(
        "thd,khd->htk", grad_heads, value_heads, preferred_element_type=jnp.float32
    )
    return (scores, grad_probs)


def block_weights(scores, grad_probs, log_total, row_delta):
    probs = jnp.exp(scores - log_total[:, :, None])
    grad_scores = probs * (grad_probs - row_delta[:, :, None])
    return (probs.astype(jnp.bfloat16), grad_scores.astype(jnp.bfloat16))


def finish_norm(inverse_norm, unit_rows, unit_grad, mean_rows):
    return (inverse_norm * (unit_grad - unit_rows * mean_rows[:, None])).astype(jnp.bfloat16)


def gathered_blocks(tp_size, query_proj, key_proj, value_proj, query_gain, key_gain, stripe_of, grad_out):
    token_count, local_width = query_proj.shape
    local_heads = local_width // HD
    width = local_width * tp_size
    stripe = token_count // 2
    device = lax.axis_index("ctx")
    query_rows = query_proj.astype(jnp.float32)
    key_rows = key_proj.astype(jnp.float32)
    query_square, key_square = lax.psum(
        (jnp.sum(query_rows * query_rows, axis=1), jnp.sum(key_rows * key_rows, axis=1)), "tp"
    )
    query_inverse = lax.rsqrt(query_square / width + EPSILON)[:, None]
    key_inverse = lax.rsqrt(key_square / width + EPSILON)[:, None]
    query_unit = query_rows * query_inverse
    key_unit = key_rows * key_inverse
    query_normed = (query_unit * query_gain).astype(jnp.bfloat16)
    key_normed = (key_unit * key_gain).astype(jnp.bfloat16)
    query_places = row_positions(stripe_of, device * token_count, token_count, stripe)
    query_heads = query_normed.reshape(token_count, local_heads, HD)
    grad_heads = grad_out.reshape(token_count, local_heads, HD)
    key_heads = key_normed.reshape(token_count, local_heads, HD)
    value_heads = value_proj.reshape(token_count, local_heads, HD)
    start_best = jnp.full((local_heads, token_count), -1e30, jnp.float32)
    zero_rows = jnp.zeros((local_heads, token_count), jnp.float32)
    key_piece = lax.all_gather(key_normed, "ctx", axis=0, tiled=True)
    value_piece = lax.all_gather(value_proj, "ctx", axis=0, tiled=True)
    row_count = key_piece.shape[0]
    block = math.gcd(row_count, 512)
    key_blocks = key_piece.reshape(row_count // block, block, local_heads, HD)
    value_blocks = value_piece.reshape(row_count // block, block, local_heads, HD)

    def forward_advance(status, entry):
        row_best, row_total, weighted = status
        key_block, value_block, block_index = entry
        key_places = row_positions(stripe_of, block_index * block, block, stripe)
        scores, grad_probs = block_scores(
            query_heads, grad_heads, query_places, key_block, value_block, key_places
        )
        new_best = jnp.maximum(row_best, jnp.max(scores, axis=2))
        decay_factor = jnp.exp(row_best - new_best)
        exponent = jnp.exp(scores - new_best[:, :, None])
        return (
            (
                new_best,
                row_total * decay_factor + jnp.sum(exponent, axis=2),
                weighted * decay_factor + jnp.sum(exponent * grad_probs, axis=2),
            ),
            None,
        )

    block_ids = jnp.arange(row_count // block, dtype=jnp.int32)
    row_best, row_total, weighted = lax.scan(
        forward_advance, (start_best, zero_rows, zero_rows), (key_blocks, value_blocks, block_ids)
    )[0]
    log_total = row_best + jnp.log(row_total)
    row_delta = weighted / row_total
    zero_grads = jnp.zeros((token_count, local_heads, HD), jnp.float32)
    total_all, delta_all = (
        lax.all_gather(log_total, "ctx", axis=1, tiled=True),
        lax.all_gather(row_delta, "ctx", axis=1, tiled=True),
    )

    def query_fold(carry_state, pieces):
        query_piece, grad_piece = pieces
        row_count = query_piece.shape[0]
        block = math.gcd(row_count, 512)
        query_blocks = query_piece.reshape(row_count // block, block, local_heads, HD)
        grad_blocks = grad_piece.reshape(row_count // block, block, local_heads, HD)

        def query_advance(status, entry):
            key_grad, value_grad = status
            query_block, grad_block, block_index = entry
            first_row = block_index * block
            block_places = row_positions(stripe_of, first_row, block, stripe)
            block_total = lax.dynamic_slice_in_dim(total_all, first_row, block, 1)
            block_delta = lax.dynamic_slice_in_dim(delta_all, first_row, block, 1)
            scores, grad_probs = block_scores(
                query_block, grad_block, block_places, key_heads, value_heads, query_places
            )
            probs_rounded, scores_rounded = block_weights(
                scores, grad_probs, block_total, block_delta
            )
            value_grad = value_grad + jnp.einsum(
                "htk,thd->khd", probs_rounded, grad_block, preferred_element_type=jnp.float32
            )
            key_grad = key_grad + jnp.einsum(
                "htk,thd->khd", scores_rounded, query_block, preferred_element_type=jnp.float32
            )
            return ((key_grad, value_grad), None)

        block_ids = jnp.arange(row_count // block, dtype=jnp.int32)
        return lax.scan(query_advance, carry_state, (query_blocks, grad_blocks, block_ids))[0]

    key_grad, value_grad = query_fold(
        (zero_grads, zero_grads),
        (
            lax.all_gather(query_normed, "ctx", axis=0, tiled=True),
            lax.all_gather(grad_out, "ctx", axis=0, tiled=True),
        ),
    )

    def key_fold(carry_state, pieces):
        key_piece, value_piece = pieces
        row_count = key_piece.shape[0]
        block = math.gcd(row_count, 512)
        key_blocks = key_piece.reshape(row_count // block, block, local_heads, HD)
        value_blocks = value_piece.reshape(row_count // block, block, local_heads, HD)

        def key_advance(query_grad, entry):
            key_block, value_block, block_index = entry
            key_places = row_positions(stripe_of, block_index * block, block, stripe)
            scores, grad_probs = block_scores(
                query_heads, grad_heads, query_places, key_block, value_block, key_places
            )
            probs_rounded, scores_rounded = block_weights(scores, grad_probs, log_total, row_delta)
            query_grad = query_grad + jnp.einsum(
                "htk,khd->thd", scores_rounded, key_block, preferred_element_type=jnp.float32
            )
            return (query_grad, None)

        block_ids = jnp.arange(row_count // block, dtype=jnp.int32)
        return lax.scan(key_advance, carry_state, (key_blocks, value_blocks, block_ids))[0]

    query_grad = key_fold(
        zero_grads,
        (
            lax.all_gather(key_normed, "ctx", axis=0, tiled=True),
            lax.all_gather(value_proj, "ctx", axis=0, tiled=True),
        ),
    )
    inverse_root = HD ** (-0.5)
    query_normed_grad = (query_grad * inverse_root).reshape(token_count, local_width)
    key_normed_grad = (key_grad * inverse_root).reshape(token_count, local_width)
    grad_value = value_grad.reshape(token_count, local_width).astype(jnp.bfloat16)
    query_unit_grad = query_normed_grad * query_gain
    key_unit_grad = key_normed_grad * key_gain
    query_mean_terms, key_mean_terms = lax.psum(
        (jnp.sum(query_unit_grad * query_unit, axis=1), jnp.sum(key_unit_grad * key_unit, axis=1)),
        "tp",
    )
    grad_query = finish_norm(query_inverse, query_unit, query_unit_grad, query_mean_terms / width)
    grad_key = finish_norm(key_inverse, key_unit, key_unit_grad, key_mean_terms / width)
    grad_query_gain, grad_key_gain = lax.psum(
        (
            jnp.sum(query_normed_grad * query_unit, axis=0),
            jnp.sum(key_normed_grad * key_unit, axis=0),
        ),
        "ctx",
    )
    return (grad_query, grad_key, grad_value, grad_query_gain, grad_key_gain)


def solution(mesh):
    peers, tp_size = mesh.shape["ctx"], mesh.shape["tp"]

    def per_device(query_proj, *others):
        local_heads = query_proj.shape[1] // HD
        whole = local_heads == peers and peers & (peers - 1) == 0 and tp_size & (tp_size - 1) == 0
        plan = functools.partial(whole_heads, peers) if whole else gathered_blocks
        return plan(tp_size, query_proj, *others)

    placed = (P("ctx", "tp"), P("ctx", "tp"), P("ctx", "tp"), P("tp"), P("tp"), P(), P("ctx", "tp"))
    return jax.shard_map(
        per_device,
        mesh=mesh,
        in_specs=placed,
        out_specs=(P("ctx", "tp"), P("ctx", "tp"), P("ctx", "tp"), P("tp"), P("tp")),
        check_vma=False,
    )
```

```python
import functools
import math

import jax
import jax.numpy as jnp
from jax import lax
from jax.experimental import pallas as pl
from jax.experimental.pallas import tpu as pltpu
from jax.sharding import PartitionSpec as P

HD = 128
EPSILON = 1e-06
VMEM = pl.BlockSpec(memory_space=pltpu.VMEM)
SMEM = pl.BlockSpec(memory_space=pltpu.SMEM)
HBM = pl.BlockSpec(memory_space=pltpu.HBM)
ANY = pl.BlockSpec(memory_space=pl.ANY)
ROWS_BY_ROWS = (((1,), (1,)), ((), ()))
COLUMNS_BY_COLUMNS = (((0,), (0,)), ((), ()))


def head_columns(head):
    return pl.ds(pl.multiple_of(head * HD, HD), HD)


def down_rows(row_vector):
    return jnp.broadcast_to(row_vector, (HD, row_vector.shape[1])).T


def lane_sums(rows):
    count = rows.shape[0]
    sums = jnp.broadcast_to(jnp.sum(rows, axis=1, keepdims=True), rows.shape)
    pieces = []
    for start in range(0, count, HD):
        size = min(HD, count - start)
        shape = (size, HD)
        mine = lax.broadcasted_iota(jnp.int32, shape, 0) == lax.broadcasted_iota(jnp.int32, shape, 1)
        piece = jnp.sum(jnp.where(mine, sums[start : start + size], 0.0), axis=0, keepdims=True)
        pieces.append(piece[:, :size])
    return jnp.concatenate(pieces, axis=1)


def cut_kernel(peers, *refs):
    in_refs, gain_refs, stripe_ref, refs = refs[:4], refs[4:6], refs[6], refs[7:]
    out_refs, (squares_ref, gains_ref, numbers_ref, sems) = refs[: 2 * peers], refs[2 * peers :]
    device = lax.axis_index("ctx")
    loads, small_loads = [], []
    for side, ref in enumerate(gain_refs):
        load = pltpu.make_async_copy(ref, gains_ref.at[side : side + 1], sems.at[4 * peers + side])
        load.start()
        small_loads.append(load)
    load = pltpu.make_async_copy(stripe_ref, numbers_ref, sems.at[4 * peers + 2])
    load.start()
    small_loads.append(load)
    for index, ref in enumerate(in_refs):
        for mask in range(peers):
            load = pltpu.make_async_copy(
                ref.at[:, head_columns(device ^ mask)],
                out_refs[index // 2 * peers + mask].at[index % 2],
                sems.at[index * peers + mask],
            )
            load.start()
            loads.append(load)
    for side in range(2):
        folded = None
        for mask in range(peers):
            loads[side * peers + mask].wait()
            rows = out_refs[mask][side].astype(jnp.float32)
            folded = rows * rows if folded is None else folded + rows * rows
        squares_ref[side : side + 1, :] = jnp.sum(folded.T, axis=0, keepdims=True)
    for load in loads[2 * peers :] + small_loads:
        load.wait()


def stripe_rows(numbers_ref, device, high, stripe):
    first, second = numbers_ref[2 * device], numbers_ref[2 * device + 1]
    number = jnp.maximum(first, second) if high else jnp.minimum(first, second)
    slot = jnp.where(second == number, 1, 0)
    place = pl.ds(pl.multiple_of(number * stripe, stripe), stripe)
    return place, pl.ds(pl.multiple_of(slot * stripe, stripe), stripe), slot


def high_rows(place, rows):
    return pl.ds(pl.multiple_of(place.start - rows // 2, place.size), place.size)


def normalize_kernel(peers, width, members, numbers_ref, gains_ref, *refs):
    parts, raw_refs = refs[:members], refs[members : members + peers]
    low_refs, high_refs = refs[members + peers : members + 2 * peers], refs[members + 2 * peers : members + 3 * peers]
    total_ref, scale_ref = refs[members + 3 * peers :]
    total = parts[0][...]
    for ref in parts[1:]:
        total = total + ref[...]
    total_ref[...] = total
    inverse = lax.rsqrt(total / width + EPSILON)
    device = lax.axis_index("ctx")
    stripe = total.shape[1] // 2
    for side in range(2):
        scale_ref[side] = down_rows(inverse[side : side + 1, :])
        for out_refs, high in ((low_refs, False), (high_refs, True)):
            _, local, _ = stripe_rows(numbers_ref, device, high, stripe)
            for mask in range(peers):
                gain = gains_ref[side : side + 1, head_columns(device ^ mask)]
                unit = raw_refs[mask][side, local, :].astype(jnp.float32) * scale_ref[side, local, :]
                out_refs[mask][side] = (unit * gain).astype(jnp.bfloat16)


def tile_rows(index, other, block):
    start = (index * (index + 1) // 2 + other) * block
    return slice(start, start + block)


def grad_probs_kernel(peers, block, numbers_ref, *refs):
    plain_refs, (grad, tiles_ref, value) = refs[:peers], refs[peers:]
    rows = grad.shape[0]
    device = lax.axis_index("ctx")
    for mask in range(peers):
        for high in (False, True):
            place, local, _ = stripe_rows(numbers_ref, device ^ mask, high, rows // (2 * peers))
            value[place, :] = plain_refs[mask][0, local, :]
            grad[place, :] = plain_refs[mask][1, local, :]
    for index in range(rows // block):
        grad_block = grad[index * block : (index + 1) * block, :]
        for other in range(index + 1):
            tiles_ref[tile_rows(index, other, block), :] = lax.dot_general(
                value[other * block : (other + 1) * block, :],
                grad_block,
                ROWS_BY_ROWS,
                preferred_element_type=jnp.float32,
            )


def column_part(tile, reduce):
    return reduce(tile.reshape(tile.shape[0] // 8, 8, tile.shape[1]), axis=0)


def in_turn(first, second):
    steps = [((index + 0.5) / len(part), step) for part in (first, second) for index, step in enumerate(part)]
    for _, step in sorted(steps, key=lambda entry: entry[0]):
        step()


def query_blocks(block, indices, query, key, grad, grad_probs, scores, probs, grad_scores, on_query, on_key):
    base, chunk = indices[-1], block // 2
    exponent_scale = HD ** (-0.5) * math.log2(math.e)
    down = lax.broadcasted_iota(jnp.int32, (chunk, block), 0)
    across = lax.broadcasted_iota(jnp.int32, (chunk, block), 1)
    best, total, delta = {}, {}, {}

    def rows_of(index):
        return slice(index * block, (index + 1) * block)

    def merge(table, index, part, join):
        table[index] = join(table[index], part) if index in table else part

    def score_steps(index):
        held = scores.at[index % 2]

        def step(start):
            tile = lax.dot_general(
                key[start : start + chunk, :],
                query[rows_of(index - base), :],
                ROWS_BY_ROWS,
                preferred_element_type=jnp.float32,
            )
            if start >= index * block:
                tile = jnp.where(down + (start - index * block) <= across, tile, -jnp.inf)
            held[start : start + chunk, :] = tile
            merge(best, index, column_part(tile, jnp.max), jnp.maximum)

        return [functools.partial(step, start) for start in range(0, (index + 1) * block, chunk)]

    def softmax_steps(index):
        held = scores.at[index % 2]

        def sums_step(start):
            if start == 0:
                best[index] = jnp.max(best[index], axis=0, keepdims=True)
            there = slice(start, start + chunk)
            tile = jnp.exp2((held[there, :] - best[index]) * exponent_scale)
            held[there, :] = tile
            merge(total, index, column_part(tile, jnp.sum), jnp.add)
            first = tile_rows(index, 0, block).start + start
            merge(delta, index, column_part(tile * grad_probs[first : first + chunk, :], jnp.sum), jnp.add)

        def rounding_step(start):
            if start == 0:
                total[index] = 1.0 / jnp.sum(total[index], axis=0, keepdims=True)
                delta[index] = jnp.sum(delta[index], axis=0, keepdims=True) * total[index]
            there, columns = slice(start, start + chunk), rows_of(index - base)
            tile = held[there, :] * total[index]
            probs[there, columns] = tile.astype(jnp.bfloat16)
            first = tile_rows(index, 0, block).start + start
            tile = tile * (grad_probs[first : first + chunk, :] - delta[index])
            grad_scores[there, columns] = tile.astype(jnp.bfloat16)

        starts = range(0, (index + 1) * block, chunk)
        return [functools.partial(step, start) for step in (sums_step, rounding_step) for start in starts]

    def product_steps(index):
        def query_step():
            seen = slice(0, (index + 1) * block)
            on_query(
                rows_of(index - base),
                lax.dot_general(
                    grad_scores[seen, rows_of(index - base)],
                    key[seen, :],
                    COLUMNS_BY_COLUMNS,
                    preferred_element_type=jnp.float32,
                ),
            )

        def key_step(other):
            columns = slice((max(index, other) - base) * block, query.shape[0])
            products = [
                jnp.dot(left[rows_of(other), columns], right[columns, :], preferred_element_type=jnp.float32)
                for left, right in ((grad_scores, query), (probs, grad))
            ]
            on_key(rows_of(other), *products)

        final = range(index, -1, -1) if index == base else [index]
        return [query_step] + [functools.partial(key_step, other) for other in final]

    for step in score_steps(indices[0]):
        step()
    products = []
    for position, index in enumerate(indices):
        following = score_steps(indices[position + 1]) if position + 1 < len(indices) else []
        in_turn(softmax_steps(index), products + following)
        products = product_steps(index)
    for step in products:
        step()


def low_kernel(peers, block, numbers_ref, grad, grad_probs, *refs):
    normed_refs, refs = refs[:peers], refs[peers:]
    query, key, query_out, key_part, value_part, sums_ref, gain_ref, query_grad, scores, probs, grad_scores = refs
    low = query.shape[0]
    stripe = low // peers
    device = lax.axis_index("ctx")
    for mask in range(peers):
        place, _, _ = stripe_rows(numbers_ref, device ^ mask, False, stripe)
        query[place, :] = normed_refs[mask][0]
        key[place, :] = normed_refs[mask][1]

    def on_query(rows, product):
        normed_grad = product * HD ** (-0.5)
        query_out[rows, :] = normed_grad.astype(jnp.bfloat16)
        query_grad[rows, :] = normed_grad * query[rows, :].astype(jnp.float32)

    def on_key(rows, key_product, value_product):
        key_part[rows, :] = key_product
        value_part[rows, :] = value_product

    indices = range(low // block - 1, -1, -1)
    query_blocks(
        block, indices, query, key, grad.at[:low], grad_probs, scores, probs, grad_scores, on_query, on_key
    )
    gain = None
    for mask in range(peers):
        place, _, _ = stripe_rows(numbers_ref, device ^ mask, False, stripe)
        terms = query_grad[place, :]
        sums_ref[mask : mask + 1, :] = lane_sums(terms)
        part = jnp.sum(terms, axis=0, keepdims=True)
        gain = part if gain is None else gain + part
    gain_ref[...] = gain


def high_kernel(peers, block, numbers_ref, grad, grad_probs, *refs):
    normed_refs, refs = refs[:peers], refs[peers:]
    _, low_key, low_query_grad, low_key_part, low_value_part, low_sums, low_gain = refs[:7]
    grads_refs, refs = refs[7 : 7 + peers], refs[7 + peers :]
    sums_ref, gain_sums_ref, query, key, query_grad, key_grad, value_grad, scores, probs, grad_scores = refs
    rows = key.shape[0]
    low = rows // 2
    stripe = low // peers
    device = lax.axis_index("ctx")
    key[:low, :] = low_key[...]
    for mask in range(peers):
        place, _, _ = stripe_rows(numbers_ref, device ^ mask, True, stripe)
        query[high_rows(place, rows), :] = normed_refs[mask][0]
        key[place, :] = normed_refs[mask][1]

    def on_query(there, product):
        query_grad[there, :] = product * HD ** (-0.5)

    def on_key(there, key_product, value_product):
        if there.start < low:
            key_product = key_product + low_key_part[there, :]
            value_product = value_product + low_value_part[there, :]
        key_grad[there, :] = key_product * HD ** (-0.5)
        value_grad[there, :] = value_product.astype(jnp.bfloat16)

    indices = range(rows // block - 1, low // block - 1, -1)
    query_blocks(
        block, indices, query, key, grad.at[low:], grad_probs, scores, probs, grad_scores, on_query, on_key
    )
    gains, sums = [low_gain[...], None], {}

    def finished(side, terms):
        part = jnp.sum(terms, axis=0, keepdims=True)
        gains[side] = part if gains[side] is None else gains[side] + part
        return lane_sums(terms)

    for high in (True, False):
        for mask in range(peers):
            place, local, _ = stripe_rows(numbers_ref, device ^ mask, high, stripe)
            normed_grad = key_grad[place, :]
            grads_refs[mask][1, local, :] = normed_grad.astype(jnp.bfloat16)
            sums[mask, 1, high] = finished(1, normed_grad * key[place, :].astype(jnp.float32))
            grads_refs[mask][2, local, :] = value_grad[place, :]
            if high:
                upper = high_rows(place, rows)
                normed_grad = query_grad[upper, :]
                grads_refs[mask][0, local, :] = normed_grad.astype(jnp.bfloat16)
                sums[mask, 0, high] = finished(0, normed_grad * query[upper, :].astype(jnp.float32))
            else:
                grads_refs[mask][0, local, :] = low_query_grad[place, :]
                sums[mask, 0, high] = low_sums[mask : mask + 1, :]
    for mask in range(peers):
        _, _, slot = stripe_rows(numbers_ref, device ^ mask, True, stripe)
        for side in range(2):
            low_row, high_row = sums[mask, side, False], sums[mask, side, True]
            row = jnp.where(
                slot == 1,
                jnp.concatenate([low_row, high_row], axis=1),
                jnp.concatenate([high_row, low_row], axis=1),
            )
            sums_ref[2 * mask + side : 2 * mask + side + 1, :] = row
    for side in range(2):
        gain_sums_ref[side : side + 1, :] = gains[side]


def totals_kernel(peers, members, gain_sums_ref, *refs):
    out_refs = refs[members:]
    total = refs[0][...]
    for ref in refs[1:members]:
        total = total + ref[...]
    for mask in range(peers):
        out_refs[mask][0:2, :] = total[2 * mask : 2 * mask + 2]
        for side in range(2):
            out_refs[mask][2 + side : 3 + side, :HD] = gain_sums_ref[side : side + 1, :]


def finish_kernel(peers, width, squares_ref, gains_ref, *refs):
    raw_refs, refs = refs[:peers], refs[peers:]
    grads_refs, sums_refs = refs[:peers], refs[peers : 2 * peers]
    out_refs, gain_out_refs = refs[2 * peers : 2 * peers + 3], refs[2 * peers + 3 : 2 * peers + 5]
    outs, out_sems = refs[2 * peers + 5 :]
    device = lax.axis_index("ctx")
    stores = []

    def store(side, mask):
        columns = head_columns(device ^ mask)
        source = grads_refs[mask].at[2] if side == 2 else outs.at[side, mask]
        copy = pltpu.make_async_copy(
            source, out_refs[side].at[:, columns], out_sems.at[side * peers + mask]
        )
        copy.start()
        stores.append(copy)

    for mask in range(peers):
        store(2, mask)
    sums = sums_refs[0][...]
    for mask in range(1, peers):
        sums = sums + sums_refs[mask][...]
    means = sums[0:2] / width
    inverse = lax.rsqrt(squares_ref[...] / width + EPSILON)
    for side in range(2):
        scale = down_rows(inverse[side : side + 1, :])
        drop = scale * down_rows(means[side : side + 1, :])
        for mask in range(peers):
            columns = head_columns(device ^ mask)
            gain = gains_ref[side : side + 1, columns]
            unit_grad = grads_refs[mask][side].astype(jnp.float32) * gain
            centered = unit_grad - raw_refs[mask][side].astype(jnp.float32) * drop
            outs[side, mask] = (scale * centered).astype(jnp.bfloat16)
            store(side, mask)
            gain_out_refs[side][:, columns] = sums_refs[mask][2 + side : 3 + side, :HD] / gain
    for copy in stores:
        copy.wait()


def swap(array, axis, size, mask):
    return lax.ppermute(array, axis, [(index, index ^ mask) for index in range(size)])


def tp_parts(array, size):
    array = array + swap(array, "tp", size, 1)
    return [array] + [swap(array, "tp", size, mask) for mask in range(2, size, 2)]


def to_peers(arrays, peers):
    return [arrays[0]] + [swap(arrays[mask], "ctx", peers, mask) for mask in range(1, peers)]


def in_hbm(array):
    return pltpu.with_memory_space_constraint(array, pltpu.HBM)


def call(kernel, out_shape, operands, in_specs, out_specs, scratch_shapes, vmem_mib):
    return pl.pallas_call(
        kernel,
        out_shape=out_shape,
        in_specs=in_specs,
        out_specs=out_specs,
        scratch_shapes=scratch_shapes,
        compiler_params=pltpu.CompilerParams(vmem_limit_bytes=vmem_mib << 20),
    )(*operands)


def whole_heads(peers, tp_size, query_proj, key_proj, value_proj, query_gain, key_gain, stripe_of, grad_out):
    token_count, local_width = query_proj.shape
    width = local_width * tp_size
    rows = token_count * peers
    members = tp_size // 2
    block = math.gcd(rows // 2, 256)
    count = rows // block
    tiles = count * (count + 1) // 2
    shape, semaphores = jax.ShapeDtypeStruct, pltpu.SemaphoreType.DMA
    head = lambda parts: shape((parts, token_count, HD), jnp.bfloat16)
    *blocks, squares, gains, numbers = call(
        functools.partial(cut_kernel, peers),
        [head(2)] * (2 * peers)
        + [
            shape((2, token_count), jnp.float32),
            shape((2, local_width), jnp.float32),
            shape(stripe_of.shape, jnp.int32),
        ],
        [
            in_hbm(array)
            for array in (query_proj, key_proj, value_proj, grad_out, query_gain[None], key_gain[None], stripe_of)
        ],
        [HBM] * 7,
        [VMEM] * (2 * peers + 3),
        [semaphores((4 * peers + 3,))],
        8,
    )
    raw, plain = blocks[:peers], to_peers(blocks[peers:], peers)
    half = shape((2, token_count // 2, HD), jnp.bfloat16)
    *normed, squares = call(
        functools.partial(normalize_kernel, peers, width, members),
        [half] * (2 * peers) + [shape((2, token_count), jnp.float32)],
        (numbers, gains, *tp_parts(squares, tp_size), *raw),
        [SMEM] + [VMEM] * (1 + members + peers),
        [VMEM] * (2 * peers + 1),
        [pltpu.VMEM((2, token_count, HD), jnp.float32)],
        8,
    )
    low_normed = to_peers(normed[:peers], peers)
    high_normed = to_peers(normed[peers:], peers)
    whole_head = shape((rows, HD), jnp.bfloat16)
    grad, grad_probs = call(
        functools.partial(grad_probs_kernel, peers, block),
        [whole_head, shape((tiles * block, block), jnp.float32)],
        (numbers, *plain),
        [SMEM] + [VMEM] * peers,
        [VMEM] * 2,
        [pltpu.VMEM((rows, HD), jnp.bfloat16)],
        8,
    )
    low = rows // 2
    low_head = lambda dtype: shape((low, HD), dtype)
    scratch = lambda keys, queries: [
        pltpu.VMEM((2, keys, block), jnp.float32),
        pltpu.VMEM((keys, queries), jnp.bfloat16),
        pltpu.VMEM((keys, queries), jnp.bfloat16),
    ]
    low_results = call(
        functools.partial(low_kernel, peers, block),
        [low_head(jnp.bfloat16)] * 3
        + [low_head(jnp.float32)] * 2
        + [shape((peers, token_count // 2), jnp.float32), shape((1, HD), jnp.float32)],
        (numbers, grad, grad_probs, *low_normed),
        [SMEM] + [VMEM] * (2 + peers),
        [VMEM] * 7,
        [pltpu.VMEM((low, HD), jnp.float32)] + scratch(low, low),
        16,
    )
    *grads, sums, gain_sums = call(
        functools.partial(high_kernel, peers, block),
        [head(3)] * peers + [shape((2 * peers, token_count), jnp.float32), shape((2, HD), jnp.float32)],
        (numbers, grad, grad_probs, *high_normed, *low_results),
        [SMEM] + [VMEM] * (2 + peers + 7),
        [VMEM] * (peers + 2),
        [
            pltpu.VMEM((low, HD), jnp.bfloat16),
            pltpu.VMEM((rows, HD), jnp.bfloat16),
            pltpu.VMEM((low, HD), jnp.float32),
            pltpu.VMEM((rows, HD), jnp.float32),
            pltpu.VMEM((rows, HD), jnp.bfloat16),
        ]
        + scratch(rows, low),
        24,
    )
    grads = to_peers(grads, peers)
    totals = call(
        functools.partial(totals_kernel, peers, members),
        [shape((4, token_count), jnp.float32)] * peers,
        (gain_sums, *tp_parts(sums, tp_size)),
        [VMEM] * (1 + members),
        [VMEM] * peers,
        [],
        8,
    )
    totals = to_peers(totals, peers)
    whole_out = shape((token_count, local_width), jnp.bfloat16)
    row = shape((1, local_width), jnp.float32)
    grad_query, grad_key, grad_value, query_gain_grad, key_gain_grad = call(
        functools.partial(finish_kernel, peers, width),
        [whole_out] * 3 + [row] * 2,
        (squares, gains, *raw, *grads, *totals),
        [VMEM] * (2 + 3 * peers),
        [ANY] * 3 + [VMEM] * 2,
        [
            pltpu.VMEM((2, peers, token_count, HD), jnp.bfloat16),
            semaphores((3 * peers,)),
        ],
        8,
    )
    return (grad_query, grad_key, grad_value, query_gain_grad[0], key_gain_grad[0])


def row_positions(stripe_list, offset, count, stripe):
    storage_rows = offset + lax.iota(jnp.int32, count)
    stripe_ids = lax.iota(jnp.int32, stripe_list.shape[0])
    matches = (storage_rows // stripe)[:, None] == stripe_ids[None, :]
    chosen = jnp.sum(jnp.where(matches, stripe_list[None, :], 0), axis=1)
    return chosen * stripe + storage_rows % stripe


def block_scores(query_heads, grad_heads, query_places, key_heads, value_heads, key_places):
    scores = jnp.einsum(
        "thd,khd->htk", query_heads, key_heads, preferred_element_type=jnp.float32
    ) * HD ** (-0.5)
    visible = key_places[None, :] <= query_places[:, None]
    scores = jnp.where(visible[None], scores, -jnp.inf)
    grad_probs = jnp.einsum(
        "thd,khd->htk", grad_heads, value_heads, preferred_element_type=jnp.float32
    )
    return (scores, grad_probs)


def block_weights(scores, grad_probs, log_total, row_delta):
    probs = jnp.exp(scores - log_total[:, :, None])
    grad_scores = probs * (grad_probs - row_delta[:, :, None])
    return (probs.astype(jnp.bfloat16), grad_scores.astype(jnp.bfloat16))


def finish_norm(inverse_norm, unit_rows, unit_grad, mean_rows):
    return (inverse_norm * (unit_grad - unit_rows * mean_rows[:, None])).astype(jnp.bfloat16)


def gathered_blocks(tp_size, query_proj, key_proj, value_proj, query_gain, key_gain, stripe_of, grad_out):
    token_count, local_width = query_proj.shape
    local_heads = local_width // HD
    width = local_width * tp_size
    stripe = token_count // 2
    device = lax.axis_index("ctx")
    query_rows = query_proj.astype(jnp.float32)
    key_rows = key_proj.astype(jnp.float32)
    query_square, key_square = lax.psum(
        (jnp.sum(query_rows * query_rows, axis=1), jnp.sum(key_rows * key_rows, axis=1)), "tp"
    )
    query_inverse = lax.rsqrt(query_square / width + EPSILON)[:, None]
    key_inverse = lax.rsqrt(key_square / width + EPSILON)[:, None]
    query_unit = query_rows * query_inverse
    key_unit = key_rows * key_inverse
    query_normed = (query_unit * query_gain).astype(jnp.bfloat16)
    key_normed = (key_unit * key_gain).astype(jnp.bfloat16)
    query_places = row_positions(stripe_of, device * token_count, token_count, stripe)
    query_heads = query_normed.reshape(token_count, local_heads, HD)
    grad_heads = grad_out.reshape(token_count, local_heads, HD)
    key_heads = key_normed.reshape(token_count, local_heads, HD)
    value_heads = value_proj.reshape(token_count, local_heads, HD)
    start_best = jnp.full((local_heads, token_count), -1e30, jnp.float32)
    zero_rows = jnp.zeros((local_heads, token_count), jnp.float32)
    key_piece = lax.all_gather(key_normed, "ctx", axis=0, tiled=True)
    value_piece = lax.all_gather(value_proj, "ctx", axis=0, tiled=True)
    row_count = key_piece.shape[0]
    block = math.gcd(row_count, 512)
    key_blocks = key_piece.reshape(row_count // block, block, local_heads, HD)
    value_blocks = value_piece.reshape(row_count // block, block, local_heads, HD)

    def forward_advance(status, entry):
        row_best, row_total, weighted = status
        key_block, value_block, block_index = entry
        key_places = row_positions(stripe_of, block_index * block, block, stripe)
        scores, grad_probs = block_scores(
            query_heads, grad_heads, query_places, key_block, value_block, key_places
        )
        new_best = jnp.maximum(row_best, jnp.max(scores, axis=2))
        decay_factor = jnp.exp(row_best - new_best)
        exponent = jnp.exp(scores - new_best[:, :, None])
        return (
            (
                new_best,
                row_total * decay_factor + jnp.sum(exponent, axis=2),
                weighted * decay_factor + jnp.sum(exponent * grad_probs, axis=2),
            ),
            None,
        )

    block_ids = jnp.arange(row_count // block, dtype=jnp.int32)
    row_best, row_total, weighted = lax.scan(
        forward_advance, (start_best, zero_rows, zero_rows), (key_blocks, value_blocks, block_ids)
    )[0]
    log_total = row_best + jnp.log(row_total)
    row_delta = weighted / row_total
    zero_grads = jnp.zeros((token_count, local_heads, HD), jnp.float32)
    total_all, delta_all = (
        lax.all_gather(log_total, "ctx", axis=1, tiled=True),
        lax.all_gather(row_delta, "ctx", axis=1, tiled=True),
    )

    def query_fold(carry_state, pieces):
        query_piece, grad_piece = pieces
        row_count = query_piece.shape[0]
        block = math.gcd(row_count, 512)
        query_blocks = query_piece.reshape(row_count // block, block, local_heads, HD)
        grad_blocks = grad_piece.reshape(row_count // block, block, local_heads, HD)

        def query_advance(status, entry):
            key_grad, value_grad = status
            query_block, grad_block, block_index = entry
            first_row = block_index * block
            block_places = row_positions(stripe_of, first_row, block, stripe)
            block_total = lax.dynamic_slice_in_dim(total_all, first_row, block, 1)
            block_delta = lax.dynamic_slice_in_dim(delta_all, first_row, block, 1)
            scores, grad_probs = block_scores(
                query_block, grad_block, block_places, key_heads, value_heads, query_places
            )
            probs_rounded, scores_rounded = block_weights(
                scores, grad_probs, block_total, block_delta
            )
            value_grad = value_grad + jnp.einsum(
                "htk,thd->khd", probs_rounded, grad_block, preferred_element_type=jnp.float32
            )
            key_grad = key_grad + jnp.einsum(
                "htk,thd->khd", scores_rounded, query_block, preferred_element_type=jnp.float32
            )
            return ((key_grad, value_grad), None)

        block_ids = jnp.arange(row_count // block, dtype=jnp.int32)
        return lax.scan(query_advance, carry_state, (query_blocks, grad_blocks, block_ids))[0]

    key_grad, value_grad = query_fold(
        (zero_grads, zero_grads),
        (
            lax.all_gather(query_normed, "ctx", axis=0, tiled=True),
            lax.all_gather(grad_out, "ctx", axis=0, tiled=True),
        ),
    )

    def key_fold(carry_state, pieces):
        key_piece, value_piece = pieces
        row_count = key_piece.shape[0]
        block = math.gcd(row_count, 512)
        key_blocks = key_piece.reshape(row_count // block, block, local_heads, HD)
        value_blocks = value_piece.reshape(row_count // block, block, local_heads, HD)

        def key_advance(query_grad, entry):
            key_block, value_block, block_index = entry
            key_places = row_positions(stripe_of, block_index * block, block, stripe)
            scores, grad_probs = block_scores(
                query_heads, grad_heads, query_places, key_block, value_block, key_places
            )
            _, scores_rounded = block_weights(scores, grad_probs, log_total, row_delta)
            query_grad = query_grad + jnp.einsum(
                "htk,khd->thd", scores_rounded, key_block, preferred_element_type=jnp.float32
            )
            return (query_grad, None)

        block_ids = jnp.arange(row_count // block, dtype=jnp.int32)
        return lax.scan(key_advance, carry_state, (key_blocks, value_blocks, block_ids))[0]

    query_grad = key_fold(
        zero_grads,
        (
            lax.all_gather(key_normed, "ctx", axis=0, tiled=True),
            lax.all_gather(value_proj, "ctx", axis=0, tiled=True),
        ),
    )
    inverse_root = HD ** (-0.5)
    query_normed_grad = (query_grad * inverse_root).reshape(token_count, local_width)
    key_normed_grad = (key_grad * inverse_root).reshape(token_count, local_width)
    grad_value = value_grad.reshape(token_count, local_width).astype(jnp.bfloat16)
    query_unit_grad = query_normed_grad * query_gain
    key_unit_grad = key_normed_grad * key_gain
    query_mean_terms, key_mean_terms = lax.psum(
        (jnp.sum(query_unit_grad * query_unit, axis=1), jnp.sum(key_unit_grad * key_unit, axis=1)),
        "tp",
    )
    grad_query = finish_norm(query_inverse, query_unit, query_unit_grad, query_mean_terms / width)
    grad_key = finish_norm(key_inverse, key_unit, key_unit_grad, key_mean_terms / width)
    grad_query_gain, grad_key_gain = lax.psum(
        (
            jnp.sum(query_normed_grad * query_unit, axis=0),
            jnp.sum(key_normed_grad * key_unit, axis=0),
        ),
        "ctx",
    )
    return (grad_query, grad_key, grad_value, grad_query_gain, grad_key_gain)


def solution(mesh):
    peers, tp_size = mesh.shape["ctx"], mesh.shape["tp"]

    def per_device(query_proj, *others):
        local_heads = query_proj.shape[1] // HD
        whole = local_heads == peers and peers & (peers - 1) == 0 and tp_size & (tp_size - 1) == 0
        if not whole:
            return gathered_blocks(tp_size, query_proj, *others)
        return whole_heads(peers, tp_size, query_proj, *others)

    placed = (P("ctx", "tp"), P("ctx", "tp"), P("ctx", "tp"), P("tp"), P("tp"), P(), P("ctx", "tp"))
    return jax.shard_map(
        per_device,
        mesh=mesh,
        in_specs=placed,
        out_specs=(P("ctx", "tp"), P("ctx", "tp"), P("ctx", "tp"), P("tp"), P("tp")),
        check_vma=False,
    )
```

```python
import functools
import math

import jax
import jax.numpy as jnp
from jax import lax
from jax.experimental import pallas as pl
from jax.experimental.pallas import tpu as pltpu
from jax.sharding import PartitionSpec as P

HD = 128
EPSILON = 1e-06
VMEM = pl.BlockSpec(memory_space=pltpu.VMEM)
SMEM = pl.BlockSpec(memory_space=pltpu.SMEM)
HBM = pl.BlockSpec(memory_space=pltpu.HBM)
ANY = pl.BlockSpec(memory_space=pl.ANY)
ROWS_BY_ROWS = (((1,), (1,)), ((), ()))
COLUMNS_BY_COLUMNS = (((0,), (0,)), ((), ()))


def head_columns(head):
    return pl.ds(pl.multiple_of(head * HD, HD), HD)


def down_rows(row_vector):
    return jnp.broadcast_to(row_vector, (HD, row_vector.shape[1])).T


def lane_sums(rows):
    count = rows.shape[0]
    sums = jnp.broadcast_to(jnp.sum(rows, axis=1, keepdims=True), rows.shape)
    pieces = []
    for start in range(0, count, HD):
        size = min(HD, count - start)
        shape = (size, HD)
        mine = lax.broadcasted_iota(jnp.int32, shape, 0) == lax.broadcasted_iota(jnp.int32, shape, 1)
        piece = jnp.sum(jnp.where(mine, sums[start : start + size], 0.0), axis=0, keepdims=True)
        pieces.append(piece[:, :size])
    return jnp.concatenate(pieces, axis=1)


def cut_kernel(peers, *refs):
    in_refs, gain_refs, stripe_ref, refs = refs[:4], refs[4:6], refs[6], refs[7:]
    out_refs, (squares_ref, gains_ref, numbers_ref, sems) = refs[: 2 * peers], refs[2 * peers :]
    device = lax.axis_index("ctx")
    loads, small_loads = [], []
    for side, ref in enumerate(gain_refs):
        load = pltpu.make_async_copy(ref, gains_ref.at[side : side + 1], sems.at[4 * peers + side])
        load.start()
        small_loads.append(load)
    load = pltpu.make_async_copy(stripe_ref, numbers_ref, sems.at[4 * peers + 2])
    load.start()
    small_loads.append(load)
    for index, ref in enumerate(in_refs):
        for mask in range(peers):
            load = pltpu.make_async_copy(
                ref.at[:, head_columns(device ^ mask)],
                out_refs[index // 2 * peers + mask].at[index % 2],
                sems.at[index * peers + mask],
            )
            load.start()
            loads.append(load)
    for side in range(2):
        folded = None
        for mask in range(peers):
            loads[side * peers + mask].wait()
            rows = out_refs[mask][side].astype(jnp.float32)
            folded = rows * rows if folded is None else folded + rows * rows
        squares_ref[side : side + 1, :] = jnp.sum(folded.T, axis=0, keepdims=True)
    for load in loads[2 * peers :] + small_loads:
        load.wait()


def stripe_rows(numbers_ref, device, high, stripe):
    first, second = numbers_ref[2 * device], numbers_ref[2 * device + 1]
    number = jnp.maximum(first, second) if high else jnp.minimum(first, second)
    slot = jnp.where(second == number, 1, 0)
    place = pl.ds(pl.multiple_of(number * stripe, stripe), stripe)
    return place, pl.ds(pl.multiple_of(slot * stripe, stripe), stripe), slot


def high_rows(place, rows):
    return pl.ds(pl.multiple_of(place.start - rows // 2, place.size), place.size)


def normalize_kernel(peers, width, members, numbers_ref, gains_ref, *refs):
    parts, raw_refs = refs[:members], refs[members : members + peers]
    low_refs, high_refs = refs[members + peers : members + 2 * peers], refs[members + 2 * peers : members + 3 * peers]
    total_ref, scale_ref = refs[members + 3 * peers :]
    total = parts[0][...]
    for ref in parts[1:]:
        total = total + ref[...]
    total_ref[...] = total
    inverse = lax.rsqrt(total / width + EPSILON)
    device = lax.axis_index("ctx")
    stripe = total.shape[1] // 2
    for side in range(2):
        scale_ref[side] = down_rows(inverse[side : side + 1, :])
        for out_refs, high in ((low_refs, False), (high_refs, True)):
            _, local, _ = stripe_rows(numbers_ref, device, high, stripe)
            for mask in range(peers):
                gain = gains_ref[side : side + 1, head_columns(device ^ mask)]
                unit = raw_refs[mask][side, local, :].astype(jnp.float32) * scale_ref[side, local, :]
                out_refs[mask][side] = (unit * gain).astype(jnp.bfloat16)


def tile_rows(index, other, block):
    start = (index * (index + 1) // 2 + other) * block
    return slice(start, start + block)


def grad_probs_kernel(peers, block, numbers_ref, *refs):
    plain_refs, (grad, tiles_ref, value) = refs[:peers], refs[peers:]
    rows = grad.shape[0]
    device = lax.axis_index("ctx")
    for mask in range(peers):
        for high in (False, True):
            place, local, _ = stripe_rows(numbers_ref, device ^ mask, high, rows // (2 * peers))
            value[place, :] = plain_refs[mask][0, local, :]
            grad[place, :] = plain_refs[mask][1, local, :]
    for index in range(rows // block):
        grad_block = grad[index * block : (index + 1) * block, :]
        for other in range(index + 1):
            tiles_ref[tile_rows(index, other, block), :] = lax.dot_general(
                value[other * block : (other + 1) * block, :],
                grad_block,
                ROWS_BY_ROWS,
                preferred_element_type=jnp.float32,
            )


def column_part(tile, reduce):
    return reduce(tile.reshape(tile.shape[0] // 8, 8, tile.shape[1]), axis=0)


def in_turn(first, second):
    steps = [((index + 0.5) / len(part), step) for part in (first, second) for index, step in enumerate(part)]
    for _, step in sorted(steps, key=lambda entry: entry[0]):
        step()


def query_blocks(
    block, indices, query, key, grad, grad_probs, scores, probs, grad_scores, on_query, on_key, late_steps=()
):
    base, chunk, fine = indices[-1], block // 2, block // 4
    exponent_scale = HD ** (-0.5) * math.log2(math.e)
    down = lax.broadcasted_iota(jnp.int32, (chunk, block), 0)
    across = lax.broadcasted_iota(jnp.int32, (chunk, block), 1)
    best, total, delta = {}, {}, {}

    def rows_of(index):
        return slice(index * block, (index + 1) * block)

    def merge(table, index, part, join):
        table[index] = join(table[index], part) if index in table else part

    def score_steps(index):
        held = scores.at[index % 2]

        def step(start):
            tile = lax.dot_general(
                key[start : start + chunk, :],
                query[rows_of(index - base), :],
                ROWS_BY_ROWS,
                preferred_element_type=jnp.float32,
            )
            if start >= index * block:
                tile = jnp.where(down + (start - index * block) <= across, tile, -jnp.inf)
            held[start : start + chunk, :] = tile
            merge(best, index, column_part(tile, jnp.max), jnp.maximum)

        return [functools.partial(step, start) for start in range(0, (index + 1) * block, chunk)]

    def softmax_steps(index):
        held = scores.at[index % 2]

        def sums_step(start):
            if start == 0:
                best[index] = jnp.max(best[index], axis=0, keepdims=True)
            there = slice(start, start + fine)
            tile = jnp.exp2((held[there, :] - best[index]) * exponent_scale)
            held[there, :] = tile
            merge(total, index, column_part(tile, jnp.sum), jnp.add)
            first = tile_rows(index, 0, block).start + start
            merge(delta, index, column_part(tile * grad_probs[first : first + fine, :], jnp.sum), jnp.add)

        def rounding_step(start):
            if start == 0:
                total[index] = 1.0 / jnp.sum(total[index], axis=0, keepdims=True)
                delta[index] = jnp.sum(delta[index], axis=0, keepdims=True) * total[index]
            there, columns = slice(start, start + fine), rows_of(index - base)
            tile = held[there, :] * total[index]
            probs[there, columns] = tile.astype(jnp.bfloat16)
            first = tile_rows(index, 0, block).start + start
            tile = tile * (grad_probs[first : first + fine, :] - delta[index])
            grad_scores[there, columns] = tile.astype(jnp.bfloat16)

        starts = range(0, (index + 1) * block, fine)
        return [functools.partial(step, start) for step in (sums_step, rounding_step) for start in starts]

    def product_steps(index):
        def query_step():
            seen = slice(0, (index + 1) * block)
            on_query(
                rows_of(index - base),
                lax.dot_general(
                    grad_scores[seen, rows_of(index - base)],
                    key[seen, :],
                    COLUMNS_BY_COLUMNS,
                    preferred_element_type=jnp.float32,
                ),
            )

        def key_step(other):
            columns = slice((max(index, other) - base) * block, query.shape[0])
            products = [
                jnp.dot(left[rows_of(other), columns], right[columns, :], preferred_element_type=jnp.float32)
                for left, right in ((grad_scores, query), (probs, grad))
            ]
            on_key(rows_of(other), *products)

        final = range(index, -1, -1) if index == base else [index]
        return [query_step] + [functools.partial(key_step, other) for other in final]

    for step in score_steps(indices[0]):
        step()
    products = []
    for position, index in enumerate(indices):
        following = score_steps(indices[position + 1]) if position + 1 < len(indices) else []
        in_turn(softmax_steps(index), products + following)
        products = product_steps(index)
    for step in products[:2]:
        step()
    in_turn(products[2:], late_steps)


def low_kernel(peers, block, numbers_ref, grad, grad_probs, *refs):
    normed_refs, refs = refs[:peers], refs[peers:]
    query, key, query_out, key_part, value_part, sums_ref, gain_ref, query_grad, scores, probs, grad_scores = refs
    low = query.shape[0]
    stripe = low // peers
    device = lax.axis_index("ctx")
    for mask in range(peers):
        place, _, _ = stripe_rows(numbers_ref, device ^ mask, False, stripe)
        query[place, :] = normed_refs[mask][0]
        key[place, :] = normed_refs[mask][1]

    def on_query(rows, product):
        normed_grad = product * HD ** (-0.5)
        query_out[rows, :] = normed_grad.astype(jnp.bfloat16)
        query_grad[rows, :] = normed_grad * query[rows, :].astype(jnp.float32)

    def on_key(rows, key_product, value_product):
        key_part[rows, :] = key_product
        value_part[rows, :] = value_product

    indices = range(low // block - 1, -1, -1)
    query_blocks(
        block, indices, query, key, grad.at[:low], grad_probs, scores, probs, grad_scores, on_query, on_key
    )
    gain = None
    for mask in range(peers):
        place, _, _ = stripe_rows(numbers_ref, device ^ mask, False, stripe)
        terms = query_grad[place, :]
        sums_ref[mask : mask + 1, :] = lane_sums(terms)
        part = jnp.sum(terms, axis=0, keepdims=True)
        gain = part if gain is None else gain + part
    gain_ref[...] = gain


def high_kernel(peers, block, numbers_ref, grad, grad_probs, *refs):
    normed_refs, refs = refs[:peers], refs[peers:]
    _, low_key, low_query_grad, low_key_part, low_value_part, low_sums, low_gain = refs[:7]
    grads_refs, refs = refs[7 : 7 + peers], refs[7 + peers :]
    sums_ref, gain_sums_ref, query, key, query_grad, key_grad, value_grad, scores, probs, grad_scores = refs
    rows = key.shape[0]
    low = rows // 2
    stripe = low // peers
    device = lax.axis_index("ctx")
    key[:low, :] = low_key[...]
    for mask in range(peers):
        place, _, _ = stripe_rows(numbers_ref, device ^ mask, True, stripe)
        query[high_rows(place, rows), :] = normed_refs[mask][0]
        key[place, :] = normed_refs[mask][1]

    def on_query(there, product):
        query_grad[there, :] = product * HD ** (-0.5)

    def on_key(there, key_product, value_product):
        if there.start < low:
            key_product = key_product + low_key_part[there, :]
            value_product = value_product + low_value_part[there, :]
        key_grad[there, :] = key_product * HD ** (-0.5)
        value_grad[there, :] = value_product.astype(jnp.bfloat16)

    gains, sums = [low_gain[...], None], {}

    def finished(side, terms):
        part = jnp.sum(terms, axis=0, keepdims=True)
        gains[side] = part if gains[side] is None else gains[side] + part
        return lane_sums(terms)

    def result_step(mask, high):
        place, local, _ = stripe_rows(numbers_ref, device ^ mask, high, stripe)
        normed_grad = key_grad[place, :]
        grads_refs[mask][1, local, :] = normed_grad.astype(jnp.bfloat16)
        sums[mask, 1, high] = finished(1, normed_grad * key[place, :].astype(jnp.float32))
        grads_refs[mask][2, local, :] = value_grad[place, :]
        if high:
            upper = high_rows(place, rows)
            normed_grad = query_grad[upper, :]
            grads_refs[mask][0, local, :] = normed_grad.astype(jnp.bfloat16)
            sums[mask, 0, high] = finished(0, normed_grad * query[upper, :].astype(jnp.float32))
        else:
            grads_refs[mask][0, local, :] = low_query_grad[place, :]
            sums[mask, 0, high] = low_sums[mask : mask + 1, :]

    indices = range(rows // block - 1, low // block - 1, -1)
    query_blocks(
        block,
        indices,
        query,
        key,
        grad.at[low:],
        grad_probs,
        scores,
        probs,
        grad_scores,
        on_query,
        on_key,
        [functools.partial(result_step, mask, True) for mask in range(peers)],
    )
    for mask in range(peers):
        result_step(mask, False)
    for mask in range(peers):
        _, _, slot = stripe_rows(numbers_ref, device ^ mask, True, stripe)
        for side in range(2):
            low_row, high_row = sums[mask, side, False], sums[mask, side, True]
            row = jnp.where(
                slot == 1,
                jnp.concatenate([low_row, high_row], axis=1),
                jnp.concatenate([high_row, low_row], axis=1),
            )
            sums_ref[2 * mask + side : 2 * mask + side + 1, :] = row
    for side in range(2):
        gain_sums_ref[side : side + 1, :] = gains[side]


def totals_kernel(peers, members, gain_sums_ref, *refs):
    out_refs = refs[members:]
    total = refs[0][...]
    for ref in refs[1:members]:
        total = total + ref[...]
    for mask in range(peers):
        out_refs[mask][0:2, :] = total[2 * mask : 2 * mask + 2]
        for side in range(2):
            out_refs[mask][2 + side : 3 + side, :HD] = gain_sums_ref[side : side + 1, :]


def finish_kernel(peers, width, squares_ref, gains_ref, *refs):
    raw_refs, refs = refs[:peers], refs[peers:]
    grads_refs, sums_refs = refs[:peers], refs[peers : 2 * peers]
    out_refs, gain_out_refs = refs[2 * peers : 2 * peers + 3], refs[2 * peers + 3 : 2 * peers + 5]
    outs, out_sems = refs[2 * peers + 5 :]
    device = lax.axis_index("ctx")
    stores = []

    def store(side, mask):
        columns = head_columns(device ^ mask)
        source = grads_refs[mask].at[2] if side == 2 else outs.at[side, mask]
        copy = pltpu.make_async_copy(
            source, out_refs[side].at[:, columns], out_sems.at[side * peers + mask]
        )
        copy.start()
        stores.append(copy)

    for mask in range(peers):
        store(2, mask)
    sums = sums_refs[0][...]
    for mask in range(1, peers):
        sums = sums + sums_refs[mask][...]
    means = sums[0:2] / width
    inverse = lax.rsqrt(squares_ref[...] / width + EPSILON)
    for side in range(2):
        scale = down_rows(inverse[side : side + 1, :])
        drop = scale * down_rows(means[side : side + 1, :])
        for mask in range(peers):
            columns = head_columns(device ^ mask)
            gain = gains_ref[side : side + 1, columns]
            unit_grad = grads_refs[mask][side].astype(jnp.float32) * gain
            centered = unit_grad - raw_refs[mask][side].astype(jnp.float32) * drop
            outs[side, mask] = (scale * centered).astype(jnp.bfloat16)
            store(side, mask)
            gain_out_refs[side][:, columns] = sums_refs[mask][2 + side : 3 + side, :HD] / gain
    for copy in stores:
        copy.wait()


def swap(array, axis, size, mask):
    return lax.ppermute(array, axis, [(index, index ^ mask) for index in range(size)])


def tp_parts(array, size):
    array = array + swap(array, "tp", size, 1)
    return [array] + [swap(array, "tp", size, mask) for mask in range(2, size, 2)]


def to_peers(arrays, peers):
    return [arrays[0]] + [swap(arrays[mask], "ctx", peers, mask) for mask in range(1, peers)]


def in_hbm(array):
    return pltpu.with_memory_space_constraint(array, pltpu.HBM)


def call(kernel, out_shape, operands, in_specs, out_specs, scratch_shapes, vmem_mib):
    return pl.pallas_call(
        kernel,
        out_shape=out_shape,
        in_specs=in_specs,
        out_specs=out_specs,
        scratch_shapes=scratch_shapes,
        compiler_params=pltpu.CompilerParams(vmem_limit_bytes=vmem_mib << 20),
    )(*operands)


def whole_heads(peers, tp_size, query_proj, key_proj, value_proj, query_gain, key_gain, stripe_of, grad_out):
    token_count, local_width = query_proj.shape
    width = local_width * tp_size
    rows = token_count * peers
    members = tp_size // 2
    block = math.gcd(rows // 2, 256)
    count = rows // block
    tiles = count * (count + 1) // 2
    shape, semaphores = jax.ShapeDtypeStruct, pltpu.SemaphoreType.DMA
    head = lambda parts: shape((parts, token_count, HD), jnp.bfloat16)
    *blocks, squares, gains, numbers = call(
        functools.partial(cut_kernel, peers),
        [head(2)] * (2 * peers)
        + [
            shape((2, token_count), jnp.float32),
            shape((2, local_width), jnp.float32),
            shape(stripe_of.shape, jnp.int32),
        ],
        [
            in_hbm(array)
            for array in (query_proj, key_proj, value_proj, grad_out, query_gain[None], key_gain[None], stripe_of)
        ],
        [HBM] * 7,
        [VMEM] * (2 * peers + 3),
        [semaphores((4 * peers + 3,))],
        8,
    )
    raw, plain = blocks[:peers], to_peers(blocks[peers:], peers)
    half = shape((2, token_count // 2, HD), jnp.bfloat16)
    *normed, squares = call(
        functools.partial(normalize_kernel, peers, width, members),
        [half] * (2 * peers) + [shape((2, token_count), jnp.float32)],
        (numbers, gains, *tp_parts(squares, tp_size), *raw),
        [SMEM] + [VMEM] * (1 + members + peers),
        [VMEM] * (2 * peers + 1),
        [pltpu.VMEM((2, token_count, HD), jnp.float32)],
        8,
    )
    low_normed = to_peers(normed[:peers], peers)
    high_normed = to_peers(normed[peers:], peers)
    whole_head = shape((rows, HD), jnp.bfloat16)
    grad, grad_probs = call(
        functools.partial(grad_probs_kernel, peers, block),
        [whole_head, shape((tiles * block, block), jnp.float32)],
        (numbers, *plain),
        [SMEM] + [VMEM] * peers,
        [VMEM] * 2,
        [pltpu.VMEM((rows, HD), jnp.bfloat16)],
        8,
    )
    low = rows // 2
    low_head = lambda dtype: shape((low, HD), dtype)
    scratch = lambda keys, queries: [
        pltpu.VMEM((2, keys, block), jnp.float32),
        pltpu.VMEM((keys, queries), jnp.bfloat16),
        pltpu.VMEM((keys, queries), jnp.bfloat16),
    ]
    low_results = call(
        functools.partial(low_kernel, peers, block),
        [low_head(jnp.bfloat16)] * 3
        + [low_head(jnp.float32)] * 2
        + [shape((peers, token_count // 2), jnp.float32), shape((1, HD), jnp.float32)],
        (numbers, grad, grad_probs, *low_normed),
        [SMEM] + [VMEM] * (2 + peers),
        [VMEM] * 7,
        [pltpu.VMEM((low, HD), jnp.float32)] + scratch(low, low),
        16,
    )
    *grads, sums, gain_sums = call(
        functools.partial(high_kernel, peers, block),
        [head(3)] * peers + [shape((2 * peers, token_count), jnp.float32), shape((2, HD), jnp.float32)],
        (numbers, grad, grad_probs, *high_normed, *low_results),
        [SMEM] + [VMEM] * (2 + peers + 7),
        [VMEM] * (peers + 2),
        [
            pltpu.VMEM((low, HD), jnp.bfloat16),
            pltpu.VMEM((rows, HD), jnp.bfloat16),
            pltpu.VMEM((low, HD), jnp.float32),
            pltpu.VMEM((rows, HD), jnp.float32),
            pltpu.VMEM((rows, HD), jnp.bfloat16),
        ]
        + scratch(rows, low),
        24,
    )
    grads = to_peers(grads, peers)
    totals = call(
        functools.partial(totals_kernel, peers, members),
        [shape((4, token_count), jnp.float32)] * peers,
        (gain_sums, *tp_parts(sums, tp_size)),
        [VMEM] * (1 + members),
        [VMEM] * peers,
        [],
        8,
    )
    totals = to_peers(totals, peers)
    whole_out = shape((token_count, local_width), jnp.bfloat16)
    row = shape((1, local_width), jnp.float32)
    grad_query, grad_key, grad_value, query_gain_grad, key_gain_grad = call(
        functools.partial(finish_kernel, peers, width),
        [whole_out] * 3 + [row] * 2,
        (squares, gains, *raw, *grads, *totals),
        [VMEM] * (2 + 3 * peers),
        [ANY] * 3 + [VMEM] * 2,
        [
            pltpu.VMEM((2, peers, token_count, HD), jnp.bfloat16),
            semaphores((3 * peers,)),
        ],
        8,
    )
    return (grad_query, grad_key, grad_value, query_gain_grad[0], key_gain_grad[0])


def row_positions(stripe_list, offset, count, stripe):
    storage_rows = offset + lax.iota(jnp.int32, count)
    stripe_ids = lax.iota(jnp.int32, stripe_list.shape[0])
    matches = (storage_rows // stripe)[:, None] == stripe_ids[None, :]
    chosen = jnp.sum(jnp.where(matches, stripe_list[None, :], 0), axis=1)
    return chosen * stripe + storage_rows % stripe


def block_scores(query_heads, grad_heads, query_places, key_heads, value_heads, key_places):
    scores = jnp.einsum(
        "thd,khd->htk", query_heads, key_heads, preferred_element_type=jnp.float32
    ) * HD ** (-0.5)
    visible = key_places[None, :] <= query_places[:, None]
    scores = jnp.where(visible[None], scores, -jnp.inf)
    grad_probs = jnp.einsum(
        "thd,khd->htk", grad_heads, value_heads, preferred_element_type=jnp.float32
    )
    return (scores, grad_probs)


def block_weights(scores, grad_probs, log_total, row_delta):
    probs = jnp.exp(scores - log_total[:, :, None])
    grad_scores = probs * (grad_probs - row_delta[:, :, None])
    return (probs.astype(jnp.bfloat16), grad_scores.astype(jnp.bfloat16))


def finish_norm(inverse_norm, unit_rows, unit_grad, mean_rows):
    return (inverse_norm * (unit_grad - unit_rows * mean_rows[:, None])).astype(jnp.bfloat16)


def gathered_blocks(tp_size, query_proj, key_proj, value_proj, query_gain, key_gain, stripe_of, grad_out):
    token_count, local_width = query_proj.shape
    local_heads = local_width // HD
    width = local_width * tp_size
    stripe = token_count // 2
    device = lax.axis_index("ctx")
    query_rows = query_proj.astype(jnp.float32)
    key_rows = key_proj.astype(jnp.float32)
    query_square, key_square = lax.psum(
        (jnp.sum(query_rows * query_rows, axis=1), jnp.sum(key_rows * key_rows, axis=1)), "tp"
    )
    query_inverse = lax.rsqrt(query_square / width + EPSILON)[:, None]
    key_inverse = lax.rsqrt(key_square / width + EPSILON)[:, None]
    query_unit = query_rows * query_inverse
    key_unit = key_rows * key_inverse
    query_normed = (query_unit * query_gain).astype(jnp.bfloat16)
    key_normed = (key_unit * key_gain).astype(jnp.bfloat16)
    query_places = row_positions(stripe_of, device * token_count, token_count, stripe)
    query_heads = query_normed.reshape(token_count, local_heads, HD)
    grad_heads = grad_out.reshape(token_count, local_heads, HD)
    key_heads = key_normed.reshape(token_count, local_heads, HD)
    value_heads = value_proj.reshape(token_count, local_heads, HD)
    start_best = jnp.full((local_heads, token_count), -1e30, jnp.float32)
    zero_rows = jnp.zeros((local_heads, token_count), jnp.float32)
    key_piece = lax.all_gather(key_normed, "ctx", axis=0, tiled=True)
    value_piece = lax.all_gather(value_proj, "ctx", axis=0, tiled=True)
    row_count = key_piece.shape[0]
    block = math.gcd(row_count, 512)
    key_blocks = key_piece.reshape(row_count // block, block, local_heads, HD)
    value_blocks = value_piece.reshape(row_count // block, block, local_heads, HD)

    def forward_advance(status, entry):
        row_best, row_total, weighted = status
        key_block, value_block, block_index = entry
        key_places = row_positions(stripe_of, block_index * block, block, stripe)
        scores, grad_probs = block_scores(
            query_heads, grad_heads, query_places, key_block, value_block, key_places
        )
        new_best = jnp.maximum(row_best, jnp.max(scores, axis=2))
        decay_factor = jnp.exp(row_best - new_best)
        exponent = jnp.exp(scores - new_best[:, :, None])
        return (
            (
                new_best,
                row_total * decay_factor + jnp.sum(exponent, axis=2),
                weighted * decay_factor + jnp.sum(exponent * grad_probs, axis=2),
            ),
            None,
        )

    block_ids = jnp.arange(row_count // block, dtype=jnp.int32)
    row_best, row_total, weighted = lax.scan(
        forward_advance, (start_best, zero_rows, zero_rows), (key_blocks, value_blocks, block_ids)
    )[0]
    log_total = row_best + jnp.log(row_total)
    row_delta = weighted / row_total
    zero_grads = jnp.zeros((token_count, local_heads, HD), jnp.float32)
    total_all, delta_all = (
        lax.all_gather(log_total, "ctx", axis=1, tiled=True),
        lax.all_gather(row_delta, "ctx", axis=1, tiled=True),
    )

    def query_fold(carry_state, pieces):
        query_piece, grad_piece = pieces
        row_count = query_piece.shape[0]
        block = math.gcd(row_count, 512)
        query_blocks = query_piece.reshape(row_count // block, block, local_heads, HD)
        grad_blocks = grad_piece.reshape(row_count // block, block, local_heads, HD)

        def query_advance(status, entry):
            key_grad, value_grad = status
            query_block, grad_block, block_index = entry
            first_row = block_index * block
            block_places = row_positions(stripe_of, first_row, block, stripe)
            block_total = lax.dynamic_slice_in_dim(total_all, first_row, block, 1)
            block_delta = lax.dynamic_slice_in_dim(delta_all, first_row, block, 1)
            scores, grad_probs = block_scores(
                query_block, grad_block, block_places, key_heads, value_heads, query_places
            )
            probs_rounded, scores_rounded = block_weights(
                scores, grad_probs, block_total, block_delta
            )
            value_grad = value_grad + jnp.einsum(
                "htk,thd->khd", probs_rounded, grad_block, preferred_element_type=jnp.float32
            )
            key_grad = key_grad + jnp.einsum(
                "htk,thd->khd", scores_rounded, query_block, preferred_element_type=jnp.float32
            )
            return ((key_grad, value_grad), None)

        block_ids = jnp.arange(row_count // block, dtype=jnp.int32)
        return lax.scan(query_advance, carry_state, (query_blocks, grad_blocks, block_ids))[0]

    key_grad, value_grad = query_fold(
        (zero_grads, zero_grads),
        (
            lax.all_gather(query_normed, "ctx", axis=0, tiled=True),
            lax.all_gather(grad_out, "ctx", axis=0, tiled=True),
        ),
    )

    def key_fold(carry_state, pieces):
        key_piece, value_piece = pieces
        row_count = key_piece.shape[0]
        block = math.gcd(row_count, 512)
        key_blocks = key_piece.reshape(row_count // block, block, local_heads, HD)
        value_blocks = value_piece.reshape(row_count // block, block, local_heads, HD)

        def key_advance(query_grad, entry):
            key_block, value_block, block_index = entry
            key_places = row_positions(stripe_of, block_index * block, block, stripe)
            scores, grad_probs = block_scores(
                query_heads, grad_heads, query_places, key_block, value_block, key_places
            )
            _, scores_rounded = block_weights(scores, grad_probs, log_total, row_delta)
            query_grad = query_grad + jnp.einsum(
                "htk,khd->thd", scores_rounded, key_block, preferred_element_type=jnp.float32
            )
            return (query_grad, None)

        block_ids = jnp.arange(row_count // block, dtype=jnp.int32)
        return lax.scan(key_advance, carry_state, (key_blocks, value_blocks, block_ids))[0]

    query_grad = key_fold(
        zero_grads,
        (
            lax.all_gather(key_normed, "ctx", axis=0, tiled=True),
            lax.all_gather(value_proj, "ctx", axis=0, tiled=True),
        ),
    )
    inverse_root = HD ** (-0.5)
    query_normed_grad = (query_grad * inverse_root).reshape(token_count, local_width)
    key_normed_grad = (key_grad * inverse_root).reshape(token_count, local_width)
    grad_value = value_grad.reshape(token_count, local_width).astype(jnp.bfloat16)
    query_unit_grad = query_normed_grad * query_gain
    key_unit_grad = key_normed_grad * key_gain
    query_mean_terms, key_mean_terms = lax.psum(
        (jnp.sum(query_unit_grad * query_unit, axis=1), jnp.sum(key_unit_grad * key_unit, axis=1)),
        "tp",
    )
    grad_query = finish_norm(query_inverse, query_unit, query_unit_grad, query_mean_terms / width)
    grad_key = finish_norm(key_inverse, key_unit, key_unit_grad, key_mean_terms / width)
    grad_query_gain, grad_key_gain = lax.psum(
        (
            jnp.sum(query_normed_grad * query_unit, axis=0),
            jnp.sum(key_normed_grad * key_unit, axis=0),
        ),
        "ctx",
    )
    return (grad_query, grad_key, grad_value, grad_query_gain, grad_key_gain)


def solution(mesh):
    peers, tp_size = mesh.shape["ctx"], mesh.shape["tp"]

    def per_device(query_proj, *others):
        local_heads = query_proj.shape[1] // HD
        whole = local_heads == peers and peers & (peers - 1) == 0 and tp_size & (tp_size - 1) == 0
        if not whole:
            return gathered_blocks(tp_size, query_proj, *others)
        return whole_heads(peers, tp_size, query_proj, *others)

    placed = (P("ctx", "tp"), P("ctx", "tp"), P("ctx", "tp"), P("tp"), P("tp"), P(), P("ctx", "tp"))
    return jax.shard_map(
        per_device,
        mesh=mesh,
        in_specs=placed,
        out_specs=(P("ctx", "tp"), P("ctx", "tp"), P("ctx", "tp"), P("tp"), P("tp")),
        check_vma=False,
    )
```

```python
import functools
import math

import jax
import jax.numpy as jnp
from jax import lax
from jax.experimental import pallas as pl
from jax.experimental.pallas import tpu as pltpu
from jax.sharding import PartitionSpec as P

HD = 128
EPSILON = 1e-06
VMEM = pl.BlockSpec(memory_space=pltpu.VMEM)
HBM = pl.BlockSpec(memory_space=pltpu.HBM)
ANY = pl.BlockSpec(memory_space=pl.ANY)
ROWS_BY_ROWS = (((1,), (1,)), ((), ()))
COLUMNS_BY_COLUMNS = (((0,), (0,)), ((), ()))


def head_columns(head):
    return pl.ds(pl.multiple_of(head * HD, HD), HD)


def down_rows(row_vector):
    return jnp.broadcast_to(row_vector, (HD, row_vector.shape[1])).T


def lane_sums(rows):
    count = rows.shape[0]
    sums = jnp.broadcast_to(jnp.sum(rows, axis=1, keepdims=True), rows.shape)
    pieces = []
    for start in range(0, count, HD):
        size = min(HD, count - start)
        shape = (size, HD)
        mine = lax.broadcasted_iota(jnp.int32, shape, 0) == lax.broadcasted_iota(jnp.int32, shape, 1)
        piece = jnp.sum(jnp.where(mine, sums[start : start + size], 0.0), axis=0, keepdims=True)
        pieces.append(piece[:, :size])
    return jnp.concatenate(pieces, axis=1)


def cut_kernel(peers, *refs):
    in_refs, gain_refs, stripe_ref, refs = refs[:4], refs[4:6], refs[6], refs[7:]
    out_refs, (squares_ref, gains_ref, numbers_ref, sems) = refs[: 2 * peers], refs[2 * peers :]
    device = lax.axis_index("ctx")
    loads, small_loads = [], []
    for side, ref in enumerate(gain_refs):
        load = pltpu.make_async_copy(ref, gains_ref.at[side : side + 1], sems.at[4 * peers + side])
        load.start()
        small_loads.append(load)
    load = pltpu.make_async_copy(stripe_ref, numbers_ref, sems.at[4 * peers + 2])
    load.start()
    small_loads.append(load)
    for index, ref in enumerate(in_refs):
        for mask in range(peers):
            load = pltpu.make_async_copy(
                ref.at[:, head_columns(device ^ mask)],
                out_refs[index // 2 * peers + mask].at[index % 2],
                sems.at[index * peers + mask],
            )
            load.start()
            loads.append(load)
    for side in range(2):
        folded = None
        for mask in range(peers):
            loads[side * peers + mask].wait()
            rows = out_refs[mask][side].astype(jnp.float32)
            folded = rows * rows if folded is None else folded + rows * rows
        squares_ref[side : side + 1, :] = jnp.sum(folded.T, axis=0, keepdims=True)
    for load in loads[2 * peers :] + small_loads:
        load.wait()


def stripe_rows(numbers_ref, device, high, stripe):
    numbers = numbers_ref[...].astype(jnp.float32)
    lanes = lax.broadcasted_iota(jnp.int32, numbers.shape, 1)
    first, second = (
        jnp.sum(jnp.where(lanes == 2 * device + slot, numbers, 0.0)).astype(jnp.int32) for slot in range(2)
    )
    number = jnp.maximum(first, second) if high else jnp.minimum(first, second)
    slot = jnp.where(second == number, 1, 0)
    place = pl.ds(pl.multiple_of(number * stripe, stripe), stripe)
    return place, pl.ds(pl.multiple_of(slot * stripe, stripe), stripe), slot


def high_rows(place, rows):
    return pl.ds(pl.multiple_of(place.start - rows // 2, place.size), place.size)


def normalize_kernel(peers, width, members, numbers_ref, gains_ref, *refs):
    parts, raw_refs = refs[:members], refs[members : members + peers]
    low_refs, high_refs = refs[members + peers : members + 2 * peers], refs[members + 2 * peers : members + 3 * peers]
    total_ref, scale_ref = refs[members + 3 * peers :]
    total = parts[0][...]
    for ref in parts[1:]:
        total = total + ref[...]
    total_ref[...] = total
    inverse = lax.rsqrt(total / width + EPSILON)
    device = lax.axis_index("ctx")
    stripe = total.shape[1] // 2
    for side in range(2):
        scale_ref[side] = down_rows(inverse[side : side + 1, :])
        for out_refs, high in ((low_refs, False), (high_refs, True)):
            _, local, _ = stripe_rows(numbers_ref, device, high, stripe)
            for mask in range(peers):
                gain = gains_ref[side : side + 1, head_columns(device ^ mask)]
                unit = raw_refs[mask][side, local, :].astype(jnp.float32) * scale_ref[side, local, :]
                out_refs[mask][side] = (unit * gain).astype(jnp.bfloat16)


def tile_rows(index, other, block):
    start = (index * (index + 1) // 2 + other) * block
    return slice(start, start + block)


def grad_probs_kernel(peers, block, numbers_ref, *refs):
    plain_refs, (grad, tiles_ref, value) = refs[:peers], refs[peers:]
    rows = grad.shape[0]
    device = lax.axis_index("ctx")
    for mask in range(peers):
        for high in (False, True):
            place, local, _ = stripe_rows(numbers_ref, device ^ mask, high, rows // (2 * peers))
            value[place, :] = plain_refs[mask][0, local, :]
            grad[place, :] = plain_refs[mask][1, local, :]
    for index in range(rows // block):
        grad_block = grad[index * block : (index + 1) * block, :]
        for other in range(index + 1):
            tiles_ref[tile_rows(index, other, block), :] = lax.dot_general(
                value[other * block : (other + 1) * block, :],
                grad_block,
                ROWS_BY_ROWS,
                preferred_element_type=jnp.float32,
            )


def column_part(tile, reduce):
    return reduce(tile.reshape(tile.shape[0] // 8, 8, tile.shape[1]), axis=0)


def in_turn(first, second):
    steps = [((index + 0.5) / len(part), step) for part in (first, second) for index, step in enumerate(part)]
    for _, step in sorted(steps, key=lambda entry: entry[0]):
        step()


def query_blocks(
    block, indices, query, key, grad, grad_probs, scores, probs, grad_scores, on_query, on_key, late_steps=()
):
    base, chunk, fine = indices[-1], block // 2, block // 4
    exponent_scale = HD ** (-0.5) * math.log2(math.e)
    down = lax.broadcasted_iota(jnp.int32, (chunk, block), 0)
    across = lax.broadcasted_iota(jnp.int32, (chunk, block), 1)
    best, total, delta = {}, {}, {}

    def rows_of(index):
        return slice(index * block, (index + 1) * block)

    def merge(table, index, part, join):
        table[index] = join(table[index], part) if index in table else part

    def score_steps(index):
        held = scores.at[index % 2]

        def step(start):
            tile = lax.dot_general(
                key[start : start + chunk, :],
                query[rows_of(index - base), :],
                ROWS_BY_ROWS,
                preferred_element_type=jnp.float32,
            )
            if start >= index * block:
                tile = jnp.where(down + (start - index * block) <= across, tile, -jnp.inf)
            held[start : start + chunk, :] = tile
            merge(best, index, column_part(tile, jnp.max), jnp.maximum)

        return [functools.partial(step, start) for start in range(0, (index + 1) * block, chunk)]

    def softmax_steps(index):
        held = scores.at[index % 2]

        def sums_step(start):
            if start == 0:
                best[index] = jnp.max(best[index], axis=0, keepdims=True)
            there = slice(start, start + fine)
            tile = jnp.exp2((held[there, :] - best[index]) * exponent_scale)
            held[there, :] = tile
            merge(total, index, column_part(tile, jnp.sum), jnp.add)
            first = tile_rows(index, 0, block).start + start
            merge(delta, index, column_part(tile * grad_probs[first : first + fine, :], jnp.sum), jnp.add)

        def rounding_step(start):
            if start == 0:
                total[index] = 1.0 / jnp.sum(total[index], axis=0, keepdims=True)
                delta[index] = jnp.sum(delta[index], axis=0, keepdims=True) * total[index]
            there, columns = slice(start, start + fine), rows_of(index - base)
            tile = held[there, :] * total[index]
            probs[there, columns] = tile.astype(jnp.bfloat16)
            first = tile_rows(index, 0, block).start + start
            tile = tile * (grad_probs[first : first + fine, :] - delta[index])
            grad_scores[there, columns] = tile.astype(jnp.bfloat16)

        starts = range(0, (index + 1) * block, fine)
        return [functools.partial(step, start) for step in (sums_step, rounding_step) for start in starts]

    def product_steps(index):
        def query_step():
            seen = slice(0, (index + 1) * block)
            on_query(
                rows_of(index - base),
                lax.dot_general(
                    grad_scores[seen, rows_of(index - base)],
                    key[seen, :],
                    COLUMNS_BY_COLUMNS,
                    preferred_element_type=jnp.float32,
                ),
            )

        def key_step(other):
            columns = slice((max(index, other) - base) * block, query.shape[0])
            products = [
                jnp.dot(left[rows_of(other), columns], right[columns, :], preferred_element_type=jnp.float32)
                for left, right in ((grad_scores, query), (probs, grad))
            ]
            on_key(rows_of(other), *products)

        final = range(index, -1, -1) if index == base else [index]
        return [query_step] + [functools.partial(key_step, other) for other in final]

    for step in score_steps(indices[0]):
        step()
    products = []
    for position, index in enumerate(indices):
        following = score_steps(indices[position + 1]) if position + 1 < len(indices) else []
        in_turn(softmax_steps(index), products + following)
        products = product_steps(index)
    for step in products[:2]:
        step()
    in_turn(products[2:], late_steps)


def low_kernel(peers, block, numbers_ref, grad, grad_probs, *refs):
    normed_refs, refs = refs[:peers], refs[peers:]
    query, key, query_out, key_part, value_part, sums_ref, gain_ref, query_grad, scores, probs, grad_scores = refs
    low = query.shape[0]
    stripe = low // peers
    device = lax.axis_index("ctx")
    for mask in range(peers):
        place, _, _ = stripe_rows(numbers_ref, device ^ mask, False, stripe)
        query[place, :] = normed_refs[mask][0]
        key[place, :] = normed_refs[mask][1]

    def on_query(rows, product):
        normed_grad = product * HD ** (-0.5)
        query_out[rows, :] = normed_grad.astype(jnp.bfloat16)
        query_grad[rows, :] = normed_grad * query[rows, :].astype(jnp.float32)

    def on_key(rows, key_product, value_product):
        key_part[rows, :] = key_product
        value_part[rows, :] = value_product

    indices = range(low // block - 1, -1, -1)
    query_blocks(
        block, indices, query, key, grad.at[:low], grad_probs, scores, probs, grad_scores, on_query, on_key
    )
    gain = None
    for mask in range(peers):
        place, _, _ = stripe_rows(numbers_ref, device ^ mask, False, stripe)
        terms = query_grad[place, :]
        sums_ref[mask : mask + 1, :] = lane_sums(terms)
        part = jnp.sum(terms, axis=0, keepdims=True)
        gain = part if gain is None else gain + part
    gain_ref[...] = gain


def high_kernel(peers, block, numbers_ref, grad, grad_probs, *refs):
    normed_refs, refs = refs[:peers], refs[peers:]
    _, low_key, low_query_grad, low_key_part, low_value_part, low_sums, low_gain = refs[:7]
    grads_refs, refs = refs[7 : 7 + peers], refs[7 + peers :]
    sums_ref, gain_sums_ref, query, key, query_grad, key_grad, value_grad, scores, probs, grad_scores = refs
    rows = key.shape[0]
    low = rows // 2
    stripe = low // peers
    device = lax.axis_index("ctx")
    key[:low, :] = low_key[...]
    for mask in range(peers):
        place, _, _ = stripe_rows(numbers_ref, device ^ mask, True, stripe)
        query[high_rows(place, rows), :] = normed_refs[mask][0]
        key[place, :] = normed_refs[mask][1]

    def on_query(there, product):
        query_grad[there, :] = product * HD ** (-0.5)

    def on_key(there, key_product, value_product):
        if there.start < low:
            key_product = key_product + low_key_part[there, :]
            value_product = value_product + low_value_part[there, :]
        key_grad[there, :] = key_product * HD ** (-0.5)
        value_grad[there, :] = value_product.astype(jnp.bfloat16)

    gains, sums = [low_gain[...], None], {}

    def finished(side, terms):
        part = jnp.sum(terms, axis=0, keepdims=True)
        gains[side] = part if gains[side] is None else gains[side] + part
        return lane_sums(terms)

    def result_step(mask, high):
        place, local, _ = stripe_rows(numbers_ref, device ^ mask, high, stripe)
        normed_grad = key_grad[place, :]
        grads_refs[mask][1, local, :] = normed_grad.astype(jnp.bfloat16)
        sums[mask, 1, high] = finished(1, normed_grad * key[place, :].astype(jnp.float32))
        grads_refs[mask][2, local, :] = value_grad[place, :]
        if high:
            upper = high_rows(place, rows)
            normed_grad = query_grad[upper, :]
            grads_refs[mask][0, local, :] = normed_grad.astype(jnp.bfloat16)
            sums[mask, 0, high] = finished(0, normed_grad * query[upper, :].astype(jnp.float32))
        else:
            grads_refs[mask][0, local, :] = low_query_grad[place, :]
            sums[mask, 0, high] = low_sums[mask : mask + 1, :]

    indices = range(rows // block - 1, low // block - 1, -1)
    query_blocks(
        block,
        indices,
        query,
        key,
        grad.at[low:],
        grad_probs,
        scores,
        probs,
        grad_scores,
        on_query,
        on_key,
        [functools.partial(result_step, mask, True) for mask in range(peers)],
    )
    for mask in range(peers):
        result_step(mask, False)
    for mask in range(peers):
        _, _, slot = stripe_rows(numbers_ref, device ^ mask, True, stripe)
        for side in range(2):
            low_row, high_row = sums[mask, side, False], sums[mask, side, True]
            row = jnp.where(
                slot == 1,
                jnp.concatenate([low_row, high_row], axis=1),
                jnp.concatenate([high_row, low_row], axis=1),
            )
            sums_ref[2 * mask + side : 2 * mask + side + 1, :] = row
    for side in range(2):
        gain_sums_ref[side : side + 1, :] = gains[side]


def totals_kernel(peers, members, gain_sums_ref, *refs):
    out_refs = refs[members:]
    total = refs[0][...]
    for ref in refs[1:members]:
        total = total + ref[...]
    for mask in range(peers):
        out_refs[mask][0:2, :] = total[2 * mask : 2 * mask + 2]
        for side in range(2):
            out_refs[mask][2 + side : 3 + side, :HD] = gain_sums_ref[side : side + 1, :]


def finish_kernel(peers, width, squares_ref, gains_ref, *refs):
    raw_refs, refs = refs[:peers], refs[peers:]
    grads_refs, sums_refs = refs[:peers], refs[peers : 2 * peers]
    out_refs, gain_out_refs = refs[2 * peers : 2 * peers + 3], refs[2 * peers + 3 : 2 * peers + 5]
    outs, out_sems = refs[2 * peers + 5 :]
    device = lax.axis_index("ctx")
    stores = []

    def store(side, mask):
        columns = head_columns(device ^ mask)
        source = grads_refs[mask].at[2] if side == 2 else outs.at[side, mask]
        copy = pltpu.make_async_copy(
            source, out_refs[side].at[:, columns], out_sems.at[side * peers + mask]
        )
        copy.start()
        stores.append(copy)

    for mask in range(peers):
        store(2, mask)
    sums = sums_refs[0][...]
    for mask in range(1, peers):
        sums = sums + sums_refs[mask][...]
    means = sums[0:2] / width
    inverse = lax.rsqrt(squares_ref[...] / width + EPSILON)
    for side in range(2):
        scale = down_rows(inverse[side : side + 1, :])
        drop = scale * down_rows(means[side : side + 1, :])
        for mask in range(peers):
            columns = head_columns(device ^ mask)
            gain = gains_ref[side : side + 1, columns]
            unit_grad = grads_refs[mask][side].astype(jnp.float32) * gain
            centered = unit_grad - raw_refs[mask][side].astype(jnp.float32) * drop
            outs[side, mask] = (scale * centered).astype(jnp.bfloat16)
            store(side, mask)
            gain_out_refs[side][:, columns] = sums_refs[mask][2 + side : 3 + side, :HD] / gain
    for copy in stores:
        copy.wait()


def swap(array, axis, size, mask):
    return lax.ppermute(array, axis, [(index, index ^ mask) for index in range(size)])


def tp_parts(array, size):
    array = array + swap(array, "tp", size, 1)
    return [array] + [swap(array, "tp", size, mask) for mask in range(2, size, 2)]


def tp_halves(array, size):
    mask = 1
    while mask < size // 2:
        array = array + swap(array, "tp", size, mask)
        mask *= 2
    return [array, swap(array, "tp", size, mask)]


def to_peers(arrays, peers):
    return [arrays[0]] + [swap(arrays[mask], "ctx", peers, mask) for mask in range(1, peers)]


def in_hbm(array):
    return pltpu.with_memory_space_constraint(array, pltpu.HBM)


def call(kernel, out_shape, operands, in_specs, out_specs, scratch_shapes, vmem_mib):
    return pl.pallas_call(
        kernel,
        out_shape=out_shape,
        in_specs=in_specs,
        out_specs=out_specs,
        scratch_shapes=scratch_shapes,
        compiler_params=pltpu.CompilerParams(vmem_limit_bytes=vmem_mib << 20),
    )(*operands)


def whole_heads(peers, tp_size, query_proj, key_proj, value_proj, query_gain, key_gain, stripe_of, grad_out):
    token_count, local_width = query_proj.shape
    width = local_width * tp_size
    rows = token_count * peers
    members = tp_size // 2
    block = math.gcd(rows // 2, 256)
    count = rows // block
    tiles = count * (count + 1) // 2
    shape, semaphores = jax.ShapeDtypeStruct, pltpu.SemaphoreType.DMA
    head = lambda parts: shape((parts, token_count, HD), jnp.bfloat16)
    *blocks, squares, gains, numbers = call(
        functools.partial(cut_kernel, peers),
        [head(2)] * (2 * peers)
        + [
            shape((2, token_count), jnp.float32),
            shape((2, local_width), jnp.float32),
            shape((1, stripe_of.shape[0]), jnp.int32),
        ],
        [
            in_hbm(array)
            for array in (query_proj, key_proj, value_proj, grad_out, query_gain[None], key_gain[None], stripe_of[None])
        ],
        [HBM] * 7,
        [VMEM] * (2 * peers + 3),
        [semaphores((4 * peers + 3,))],
        8,
    )
    raw, plain = blocks[:peers], to_peers(blocks[peers:], peers)
    half = shape((2, token_count // 2, HD), jnp.bfloat16)
    *normed, squares = call(
        functools.partial(normalize_kernel, peers, width, members),
        [half] * (2 * peers) + [shape((2, token_count), jnp.float32)],
        (numbers, gains, *tp_parts(squares, tp_size), *raw),
        [VMEM] + [VMEM] * (1 + members + peers),
        [VMEM] * (2 * peers + 1),
        [pltpu.VMEM((2, token_count, HD), jnp.float32)],
        8,
    )
    low_normed = to_peers(normed[:peers], peers)
    high_normed = to_peers(normed[peers:], peers)
    whole_head = shape((rows, HD), jnp.bfloat16)
    grad, grad_probs = call(
        functools.partial(grad_probs_kernel, peers, block),
        [whole_head, shape((tiles * block, block), jnp.float32)],
        (numbers, *plain),
        [VMEM] + [VMEM] * peers,
        [VMEM] * 2,
        [pltpu.VMEM((rows, HD), jnp.bfloat16)],
        8,
    )
    low = rows // 2
    low_head = lambda dtype: shape((low, HD), dtype)
    scratch = lambda keys, queries: [
        pltpu.VMEM((2, keys, block), jnp.float32),
        pltpu.VMEM((keys, queries), jnp.bfloat16),
        pltpu.VMEM((keys, queries), jnp.bfloat16),
    ]
    low_results = call(
        functools.partial(low_kernel, peers, block),
        [low_head(jnp.bfloat16)] * 3
        + [low_head(jnp.float32)] * 2
        + [shape((peers, token_count // 2), jnp.float32), shape((1, HD), jnp.float32)],
        (numbers, grad, grad_probs, *low_normed),
        [VMEM] + [VMEM] * (2 + peers),
        [VMEM] * 7,
        [pltpu.VMEM((low, HD), jnp.float32)] + scratch(low, low),
        16,
    )
    *grads, sums, gain_sums = call(
        functools.partial(high_kernel, peers, block),
        [head(3)] * peers + [shape((2 * peers, token_count), jnp.float32), shape((2, HD), jnp.float32)],
        (numbers, grad, grad_probs, *high_normed, *low_results),
        [VMEM] + [VMEM] * (2 + peers + 7),
        [VMEM] * (peers + 2),
        [
            pltpu.VMEM((low, HD), jnp.bfloat16),
            pltpu.VMEM((rows, HD), jnp.bfloat16),
            pltpu.VMEM((low, HD), jnp.float32),
            pltpu.VMEM((rows, HD), jnp.float32),
            pltpu.VMEM((rows, HD), jnp.bfloat16),
        ]
        + scratch(rows, low),
        24,
    )
    grads = to_peers(grads, peers)
    totals = call(
        functools.partial(totals_kernel, peers, 2),
        [shape((4, token_count), jnp.float32)] * peers,
        (gain_sums, *tp_halves(sums, tp_size)),
        [VMEM] * 3,
        [VMEM] * peers,
        [],
        8,
    )
    totals = to_peers(totals, peers)
    whole_out = shape((token_count, local_width), jnp.bfloat16)
    row = shape((1, local_width), jnp.float32)
    grad_query, grad_key, grad_value, query_gain_grad, key_gain_grad = call(
        functools.partial(finish_kernel, peers, width),
        [whole_out] * 3 + [row] * 2,
        (squares, gains, *raw, *grads, *totals),
        [VMEM] * (2 + 3 * peers),
        [ANY] * 3 + [VMEM] * 2,
        [
            pltpu.VMEM((2, peers, token_count, HD), jnp.bfloat16),
            semaphores((3 * peers,)),
        ],
        8,
    )
    return (grad_query, grad_key, grad_value, query_gain_grad[0], key_gain_grad[0])


def row_positions(stripe_list, offset, count, stripe):
    storage_rows = offset + lax.iota(jnp.int32, count)
    stripe_ids = lax.iota(jnp.int32, stripe_list.shape[0])
    matches = (storage_rows // stripe)[:, None] == stripe_ids[None, :]
    chosen = jnp.sum(jnp.where(matches, stripe_list[None, :], 0), axis=1)
    return chosen * stripe + storage_rows % stripe


def block_scores(query_heads, grad_heads, query_places, key_heads, value_heads, key_places):
    scores = jnp.einsum(
        "thd,khd->htk", query_heads, key_heads, preferred_element_type=jnp.float32
    ) * HD ** (-0.5)
    visible = key_places[None, :] <= query_places[:, None]
    scores = jnp.where(visible[None], scores, -jnp.inf)
    grad_probs = jnp.einsum(
        "thd,khd->htk", grad_heads, value_heads, preferred_element_type=jnp.float32
    )
    return (scores, grad_probs)


def block_weights(scores, grad_probs, log_total, row_delta):
    probs = jnp.exp(scores - log_total[:, :, None])
    grad_scores = probs * (grad_probs - row_delta[:, :, None])
    return (probs.astype(jnp.bfloat16), grad_scores.astype(jnp.bfloat16))


def finish_norm(inverse_norm, unit_rows, unit_grad, mean_rows):
    return (inverse_norm * (unit_grad - unit_rows * mean_rows[:, None])).astype(jnp.bfloat16)


def gathered_blocks(tp_size, query_proj, key_proj, value_proj, query_gain, key_gain, stripe_of, grad_out):
    token_count, local_width = query_proj.shape
    local_heads = local_width // HD
    width = local_width * tp_size
    stripe = token_count // 2
    device = lax.axis_index("ctx")
    query_rows = query_proj.astype(jnp.float32)
    key_rows = key_proj.astype(jnp.float32)
    query_square, key_square = lax.psum(
        (jnp.sum(query_rows * query_rows, axis=1), jnp.sum(key_rows * key_rows, axis=1)), "tp"
    )
    query_inverse = lax.rsqrt(query_square / width + EPSILON)[:, None]
    key_inverse = lax.rsqrt(key_square / width + EPSILON)[:, None]
    query_unit = query_rows * query_inverse
    key_unit = key_rows * key_inverse
    query_normed = (query_unit * query_gain).astype(jnp.bfloat16)
    key_normed = (key_unit * key_gain).astype(jnp.bfloat16)
    query_places = row_positions(stripe_of, device * token_count, token_count, stripe)
    query_heads = query_normed.reshape(token_count, local_heads, HD)
    grad_heads = grad_out.reshape(token_count, local_heads, HD)
    key_heads = key_normed.reshape(token_count, local_heads, HD)
    value_heads = value_proj.reshape(token_count, local_heads, HD)
    start_best = jnp.full((local_heads, token_count), -1e30, jnp.float32)
    zero_rows = jnp.zeros((local_heads, token_count), jnp.float32)
    key_piece = lax.all_gather(key_normed, "ctx", axis=0, tiled=True)
    value_piece = lax.all_gather(value_proj, "ctx", axis=0, tiled=True)
    row_count = key_piece.shape[0]
    block = math.gcd(row_count, 512)
    key_blocks = key_piece.reshape(row_count // block, block, local_heads, HD)
    value_blocks = value_piece.reshape(row_count // block, block, local_heads, HD)

    def forward_advance(status, entry):
        row_best, row_total, weighted = status
        key_block, value_block, block_index = entry
        key_places = row_positions(stripe_of, block_index * block, block, stripe)
        scores, grad_probs = block_scores(
            query_heads, grad_heads, query_places, key_block, value_block, key_places
        )
        new_best = jnp.maximum(row_best, jnp.max(scores, axis=2))
        decay_factor = jnp.exp(row_best - new_best)
        exponent = jnp.exp(scores - new_best[:, :, None])
        return (
            (
                new_best,
                row_total * decay_factor + jnp.sum(exponent, axis=2),
                weighted * decay_factor + jnp.sum(exponent * grad_probs, axis=2),
            ),
            None,
        )

    block_ids = jnp.arange(row_count // block, dtype=jnp.int32)
    row_best, row_total, weighted = lax.scan(
        forward_advance, (start_best, zero_rows, zero_rows), (key_blocks, value_blocks, block_ids)
    )[0]
    log_total = row_best + jnp.log(row_total)
    row_delta = weighted / row_total
    zero_grads = jnp.zeros((token_count, local_heads, HD), jnp.float32)
    total_all, delta_all = (
        lax.all_gather(log_total, "ctx", axis=1, tiled=True),
        lax.all_gather(row_delta, "ctx", axis=1, tiled=True),
    )

    def query_fold(carry_state, pieces):
        query_piece, grad_piece = pieces
        row_count = query_piece.shape[0]
        block = math.gcd(row_count, 512)
        query_blocks = query_piece.reshape(row_count // block, block, local_heads, HD)
        grad_blocks = grad_piece.reshape(row_count // block, block, local_heads, HD)

        def query_advance(status, entry):
            key_grad, value_grad = status
            query_block, grad_block, block_index = entry
            first_row = block_index * block
            block_places = row_positions(stripe_of, first_row, block, stripe)
            block_total = lax.dynamic_slice_in_dim(total_all, first_row, block, 1)
            block_delta = lax.dynamic_slice_in_dim(delta_all, first_row, block, 1)
            scores, grad_probs = block_scores(
                query_block, grad_block, block_places, key_heads, value_heads, query_places
            )
            probs_rounded, scores_rounded = block_weights(
                scores, grad_probs, block_total, block_delta
            )
            value_grad = value_grad + jnp.einsum(
                "htk,thd->khd", probs_rounded, grad_block, preferred_element_type=jnp.float32
            )
            key_grad = key_grad + jnp.einsum(
                "htk,thd->khd", scores_rounded, query_block, preferred_element_type=jnp.float32
            )
            return ((key_grad, value_grad), None)

        block_ids = jnp.arange(row_count // block, dtype=jnp.int32)
        return lax.scan(query_advance, carry_state, (query_blocks, grad_blocks, block_ids))[0]

    key_grad, value_grad = query_fold(
        (zero_grads, zero_grads),
        (
            lax.all_gather(query_normed, "ctx", axis=0, tiled=True),
            lax.all_gather(grad_out, "ctx", axis=0, tiled=True),
        ),
    )

    def key_fold(carry_state, pieces):
        key_piece, value_piece = pieces
        row_count = key_piece.shape[0]
        block = math.gcd(row_count, 512)
        key_blocks = key_piece.reshape(row_count // block, block, local_heads, HD)
        value_blocks = value_piece.reshape(row_count // block, block, local_heads, HD)

        def key_advance(query_grad, entry):
            key_block, value_block, block_index = entry
            key_places = row_positions(stripe_of, block_index * block, block, stripe)
            scores, grad_probs = block_scores(
                query_heads, grad_heads, query_places, key_block, value_block, key_places
            )
            _, scores_rounded = block_weights(scores, grad_probs, log_total, row_delta)
            query_grad = query_grad + jnp.einsum(
                "htk,khd->thd", scores_rounded, key_block, preferred_element_type=jnp.float32
            )
            return (query_grad, None)

        block_ids = jnp.arange(row_count // block, dtype=jnp.int32)
        return lax.scan(key_advance, carry_state, (key_blocks, value_blocks, block_ids))[0]

    query_grad = key_fold(
        zero_grads,
        (
            lax.all_gather(key_normed, "ctx", axis=0, tiled=True),
            lax.all_gather(value_proj, "ctx", axis=0, tiled=True),
        ),
    )
    inverse_root = HD ** (-0.5)
    query_normed_grad = (query_grad * inverse_root).reshape(token_count, local_width)
    key_normed_grad = (key_grad * inverse_root).reshape(token_count, local_width)
    grad_value = value_grad.reshape(token_count, local_width).astype(jnp.bfloat16)
    query_unit_grad = query_normed_grad * query_gain
    key_unit_grad = key_normed_grad * key_gain
    query_mean_terms, key_mean_terms = lax.psum(
        (jnp.sum(query_unit_grad * query_unit, axis=1), jnp.sum(key_unit_grad * key_unit, axis=1)),
        "tp",
    )
    grad_query = finish_norm(query_inverse, query_unit, query_unit_grad, query_mean_terms / width)
    grad_key = finish_norm(key_inverse, key_unit, key_unit_grad, key_mean_terms / width)
    grad_query_gain, grad_key_gain = lax.psum(
        (
            jnp.sum(query_normed_grad * query_unit, axis=0),
            jnp.sum(key_normed_grad * key_unit, axis=0),
        ),
        "ctx",
    )
    return (grad_query, grad_key, grad_value, grad_query_gain, grad_key_gain)


def solution(mesh):
    peers, tp_size = mesh.shape["ctx"], mesh.shape["tp"]

    def per_device(query_proj, *others):
        local_heads = query_proj.shape[1] // HD
        whole = local_heads == peers and peers & (peers - 1) == 0 and tp_size & (tp_size - 1) == 0
        if not whole:
            return gathered_blocks(tp_size, query_proj, *others)
        return whole_heads(peers, tp_size, query_proj, *others)

    placed = (P("ctx", "tp"), P("ctx", "tp"), P("ctx", "tp"), P("tp"), P("tp"), P(), P("ctx", "tp"))
    return jax.shard_map(
        per_device,
        mesh=mesh,
        in_specs=placed,
        out_specs=(P("ctx", "tp"), P("ctx", "tp"), P("ctx", "tp"), P("tp"), P("tp")),
        check_vma=False,
    )
```

```python
import functools
import math

import jax
import jax.numpy as jnp
from jax import lax
from jax.experimental import pallas as pl
from jax.experimental.pallas import tpu as pltpu
from jax.sharding import PartitionSpec as P

HD = 128
EPSILON = 1e-06
VMEM = pl.BlockSpec(memory_space=pltpu.VMEM)
HBM = pl.BlockSpec(memory_space=pltpu.HBM)
ANY = pl.BlockSpec(memory_space=pl.ANY)
ROWS_BY_ROWS = (((1,), (1,)), ((), ()))
COLUMNS_BY_COLUMNS = (((0,), (0,)), ((), ()))


def head_columns(head):
    return pl.ds(pl.multiple_of(head * HD, HD), HD)


def down_rows(row_vector):
    return jnp.broadcast_to(row_vector, (HD, row_vector.shape[1])).T


def lane_sums(rows):
    count = rows.shape[0]
    sums = jnp.broadcast_to(jnp.sum(rows, axis=1, keepdims=True), rows.shape)
    pieces = []
    for start in range(0, count, HD):
        size = min(HD, count - start)
        shape = (size, HD)
        mine = lax.broadcasted_iota(jnp.int32, shape, 0) == lax.broadcasted_iota(jnp.int32, shape, 1)
        piece = jnp.sum(jnp.where(mine, sums[start : start + size], 0.0), axis=0, keepdims=True)
        pieces.append(piece[:, :size])
    return jnp.concatenate(pieces, axis=1)


def cut_kernel(peers, *refs):
    in_refs, gain_refs, stripe_ref, refs = refs[:4], refs[4:6], refs[6], refs[7:]
    out_refs, (squares_ref, gains_ref, numbers_ref, sems) = refs[: 2 * peers], refs[2 * peers :]
    device = lax.axis_index("ctx")
    loads, small_loads = [], []
    for side, ref in enumerate(gain_refs):
        load = pltpu.make_async_copy(ref, gains_ref.at[side : side + 1], sems.at[4 * peers + side])
        load.start()
        small_loads.append(load)
    load = pltpu.make_async_copy(stripe_ref, numbers_ref, sems.at[4 * peers + 2])
    load.start()
    small_loads.append(load)
    for index, ref in enumerate(in_refs):
        for mask in range(peers):
            load = pltpu.make_async_copy(
                ref.at[:, head_columns(device ^ mask)],
                out_refs[index // 2 * peers + mask].at[index % 2],
                sems.at[index * peers + mask],
            )
            load.start()
            loads.append(load)
    for side in range(2):
        folded = None
        for mask in range(peers):
            loads[side * peers + mask].wait()
            rows = out_refs[mask][side].astype(jnp.float32)
            folded = rows * rows if folded is None else folded + rows * rows
        squares_ref[side : side + 1, :] = jnp.sum(folded.T, axis=0, keepdims=True)
    for load in loads[2 * peers :] + small_loads:
        load.wait()


def stripe_rows(numbers_ref, device, high, stripe):
    numbers = numbers_ref[...].astype(jnp.float32)
    lanes = lax.broadcasted_iota(jnp.int32, numbers.shape, 1)
    first, second = (
        jnp.sum(jnp.where(lanes == 2 * device + slot, numbers, 0.0)).astype(jnp.int32) for slot in range(2)
    )
    number = jnp.maximum(first, second) if high else jnp.minimum(first, second)
    slot = jnp.where(second == number, 1, 0)
    place = pl.ds(pl.multiple_of(number * stripe, stripe), stripe)
    return place, pl.ds(pl.multiple_of(slot * stripe, stripe), stripe), slot


def high_rows(place, rows):
    return pl.ds(pl.multiple_of(place.start - rows // 2, place.size), place.size)


def normalize_kernel(peers, width, members, numbers_ref, gains_ref, *refs):
    parts, raw_refs = refs[:members], refs[members : members + peers]
    low_refs, high_refs = refs[members + peers : members + 2 * peers], refs[members + 2 * peers : members + 3 * peers]
    scale_ref = refs[members + 3 * peers]
    total = parts[0][...]
    for ref in parts[1:]:
        total = total + ref[...]
    inverse = lax.rsqrt(total / width + EPSILON)
    device = lax.axis_index("ctx")
    stripe = total.shape[1] // 2
    for side in range(2):
        scale_ref[side] = down_rows(inverse[side : side + 1, :])
        for out_refs, high in ((low_refs, False), (high_refs, True)):
            _, local, _ = stripe_rows(numbers_ref, device, high, stripe)
            for mask in range(peers):
                gain = gains_ref[side : side + 1, head_columns(device ^ mask)]
                unit = raw_refs[mask][side, local, :].astype(jnp.float32) * scale_ref[side, local, :]
                out_refs[mask][side] = (unit * gain).astype(jnp.bfloat16)


def tile_rows(index, other, block):
    start = (index * (index + 1) // 2 + other) * block
    return slice(start, start + block)


def grad_probs_kernel(peers, block, numbers_ref, *refs):
    plain_refs, (grad, tiles_ref, value) = refs[:peers], refs[peers:]
    rows = grad.shape[0]
    device = lax.axis_index("ctx")
    for mask in range(peers):
        for high in (False, True):
            place, local, _ = stripe_rows(numbers_ref, device ^ mask, high, rows // (2 * peers))
            value[place, :] = plain_refs[mask][0, local, :]
            grad[place, :] = plain_refs[mask][1, local, :]
    for index in range(rows // block):
        grad_block = grad[index * block : (index + 1) * block, :]
        for other in range(index + 1):
            tiles_ref[tile_rows(index, other, block), :] = lax.dot_general(
                value[other * block : (other + 1) * block, :],
                grad_block,
                ROWS_BY_ROWS,
                preferred_element_type=jnp.float32,
            )


def column_part(tile, reduce):
    return reduce(tile.reshape(tile.shape[0] // 8, 8, tile.shape[1]), axis=0)


def in_turn(first, second):
    steps = [((index + 0.5) / len(part), step) for part in (first, second) for index, step in enumerate(part)]
    for _, step in sorted(steps, key=lambda entry: entry[0]):
        step()


def query_blocks(
    block, indices, query, key, grad, grad_probs, scores, probs, grad_scores, on_query, on_key, late_steps=()
):
    base, chunk, fine = indices[-1], block // 2, block // 4
    exponent_scale = HD ** (-0.5) * math.log2(math.e)
    down = lax.broadcasted_iota(jnp.int32, (chunk, block), 0)
    across = lax.broadcasted_iota(jnp.int32, (chunk, block), 1)
    best, total, delta = {}, {}, {}

    def rows_of(index):
        return slice(index * block, (index + 1) * block)

    def merge(table, index, part, join):
        table[index] = join(table[index], part) if index in table else part

    def score_steps(index):
        held = scores.at[index % 2]

        def step(start):
            tile = lax.dot_general(
                key[start : start + chunk, :],
                query[rows_of(index - base), :],
                ROWS_BY_ROWS,
                preferred_element_type=jnp.float32,
            )
            if start >= index * block:
                tile = jnp.where(down + (start - index * block) <= across, tile, -jnp.inf)
            held[start : start + chunk, :] = tile
            merge(best, index, column_part(tile, jnp.max), jnp.maximum)

        return [functools.partial(step, start) for start in range(0, (index + 1) * block, chunk)]

    def softmax_steps(index):
        held = scores.at[index % 2]

        def sums_step(start):
            if start == 0:
                best[index] = jnp.max(best[index], axis=0, keepdims=True)
            there = slice(start, start + fine)
            tile = jnp.exp2((held[there, :] - best[index]) * exponent_scale)
            held[there, :] = tile
            merge(total, index, column_part(tile, jnp.sum), jnp.add)
            first = tile_rows(index, 0, block).start + start
            merge(delta, index, column_part(tile * grad_probs[first : first + fine, :], jnp.sum), jnp.add)

        def rounding_step(start):
            if start == 0:
                total[index] = 1.0 / jnp.sum(total[index], axis=0, keepdims=True)
                delta[index] = jnp.sum(delta[index], axis=0, keepdims=True) * total[index]
            there, columns = slice(start, start + fine), rows_of(index - base)
            tile = held[there, :] * total[index]
            probs[there, columns] = tile.astype(jnp.bfloat16)
            first = tile_rows(index, 0, block).start + start
            tile = tile * (grad_probs[first : first + fine, :] - delta[index])
            grad_scores[there, columns] = tile.astype(jnp.bfloat16)

        starts = range(0, (index + 1) * block, fine)
        return [functools.partial(step, start) for step in (sums_step, rounding_step) for start in starts]

    def product_steps(index):
        def query_step():
            seen = slice(0, (index + 1) * block)
            on_query(
                rows_of(index - base),
                lax.dot_general(
                    grad_scores[seen, rows_of(index - base)],
                    key[seen, :],
                    COLUMNS_BY_COLUMNS,
                    preferred_element_type=jnp.float32,
                ),
            )

        def key_step(other):
            columns = slice((max(index, other) - base) * block, query.shape[0])
            products = [
                jnp.dot(left[rows_of(other), columns], right[columns, :], preferred_element_type=jnp.float32)
                for left, right in ((grad_scores, query), (probs, grad))
            ]
            on_key(rows_of(other), *products)

        final = range(index, -1, -1) if index == base else [index]
        return [query_step] + [functools.partial(key_step, other) for other in final]

    for step in score_steps(indices[0]):
        step()
    products = []
    for position, index in enumerate(indices):
        following = score_steps(indices[position + 1]) if position + 1 < len(indices) else []
        in_turn(softmax_steps(index), products + following)
        products = product_steps(index)
    for step in products[:2]:
        step()
    in_turn(products[2:], late_steps)


def low_kernel(peers, block, numbers_ref, grad, grad_probs, *refs):
    normed_refs, refs = refs[:peers], refs[peers:]
    query, key, query_out, key_part, value_part, sums_ref, gain_ref, query_grad, scores, probs, grad_scores = refs
    low = query.shape[0]
    stripe = low // peers
    device = lax.axis_index("ctx")
    for mask in range(peers):
        place, _, _ = stripe_rows(numbers_ref, device ^ mask, False, stripe)
        query[place, :] = normed_refs[mask][0]
        key[place, :] = normed_refs[mask][1]

    def on_query(rows, product):
        normed_grad = product * HD ** (-0.5)
        query_out[rows, :] = normed_grad.astype(jnp.bfloat16)
        query_grad[rows, :] = normed_grad * query[rows, :].astype(jnp.float32)

    def on_key(rows, key_product, value_product):
        key_part[rows, :] = key_product
        value_part[rows, :] = value_product

    indices = range(low // block - 1, -1, -1)
    query_blocks(
        block, indices, query, key, grad.at[:low], grad_probs, scores, probs, grad_scores, on_query, on_key
    )
    gain = None
    for mask in range(peers):
        place, _, _ = stripe_rows(numbers_ref, device ^ mask, False, stripe)
        terms = query_grad[place, :]
        sums_ref[mask : mask + 1, :] = lane_sums(terms)
        part = jnp.sum(terms, axis=0, keepdims=True)
        gain = part if gain is None else gain + part
    gain_ref[...] = gain


def high_kernel(peers, block, numbers_ref, grad, grad_probs, *refs):
    normed_refs, refs = refs[:peers], refs[peers:]
    _, low_key, low_query_grad, low_key_part, low_value_part, low_sums, low_gain = refs[:7]
    grads_refs, refs = refs[7 : 7 + peers], refs[7 + peers :]
    sums_ref, gain_sums_ref, query, key, query_grad, key_grad, value_grad, scores, probs, grad_scores = refs
    rows = key.shape[0]
    low = rows // 2
    stripe = low // peers
    device = lax.axis_index("ctx")
    key[:low, :] = low_key[...]
    for mask in range(peers):
        place, _, _ = stripe_rows(numbers_ref, device ^ mask, True, stripe)
        query[high_rows(place, rows), :] = normed_refs[mask][0]
        key[place, :] = normed_refs[mask][1]

    def on_query(there, product):
        query_grad[there, :] = product * HD ** (-0.5)

    def on_key(there, key_product, value_product):
        if there.start < low:
            key_product = key_product + low_key_part[there, :]
            value_product = value_product + low_value_part[there, :]
        key_grad[there, :] = key_product * HD ** (-0.5)
        value_grad[there, :] = value_product.astype(jnp.bfloat16)

    gains, sums = [low_gain[...], None], {}

    def finished(side, terms):
        part = jnp.sum(terms, axis=0, keepdims=True)
        gains[side] = part if gains[side] is None else gains[side] + part
        return lane_sums(terms)

    def result_step(mask, high):
        place, local, _ = stripe_rows(numbers_ref, device ^ mask, high, stripe)
        normed_grad = key_grad[place, :]
        grads_refs[mask][1, local, :] = normed_grad.astype(jnp.bfloat16)
        sums[mask, 1, high] = finished(1, normed_grad * key[place, :].astype(jnp.float32))
        grads_refs[mask][2, local, :] = value_grad[place, :]
        if high:
            upper = high_rows(place, rows)
            normed_grad = query_grad[upper, :]
            grads_refs[mask][0, local, :] = normed_grad.astype(jnp.bfloat16)
            sums[mask, 0, high] = finished(0, normed_grad * query[upper, :].astype(jnp.float32))
        else:
            grads_refs[mask][0, local, :] = low_query_grad[place, :]
            sums[mask, 0, high] = low_sums[mask : mask + 1, :]

    indices = range(rows // block - 1, low // block - 1, -1)
    query_blocks(
        block,
        indices,
        query,
        key,
        grad.at[low:],
        grad_probs,
        scores,
        probs,
        grad_scores,
        on_query,
        on_key,
        [functools.partial(result_step, mask, True) for mask in range(peers)],
    )
    for mask in range(peers):
        result_step(mask, False)
    for mask in range(peers):
        _, _, slot = stripe_rows(numbers_ref, device ^ mask, True, stripe)
        for side in range(2):
            low_row, high_row = sums[mask, side, False], sums[mask, side, True]
            row = jnp.where(
                slot == 1,
                jnp.concatenate([low_row, high_row], axis=1),
                jnp.concatenate([high_row, low_row], axis=1),
            )
            sums_ref[2 * mask + side : 2 * mask + side + 1, :] = row
    for side in range(2):
        gain_sums_ref[side : side + 1, :] = gains[side]


def totals_kernel(peers, members, gain_sums_ref, *refs):
    out_refs = refs[members:]
    total = refs[0][...]
    for ref in refs[1:members]:
        total = total + ref[...]
    for mask in range(peers):
        out_refs[mask][0:2, :] = total[2 * mask : 2 * mask + 2]
        for side in range(2):
            out_refs[mask][2 + side : 3 + side, :HD] = gain_sums_ref[side : side + 1, :]


def finish_kernel(peers, width, scales_ref, gains_ref, *refs):
    raw_refs, refs = refs[:peers], refs[peers:]
    grads_refs, sums_refs = refs[:peers], refs[peers : 2 * peers]
    out_refs, gain_out_refs = refs[2 * peers : 2 * peers + 3], refs[2 * peers + 3 : 2 * peers + 5]
    outs, out_sems = refs[2 * peers + 5 :]
    device = lax.axis_index("ctx")
    stores = []

    def store(side, mask):
        columns = head_columns(device ^ mask)
        source = grads_refs[mask].at[2] if side == 2 else outs.at[side, mask]
        copy = pltpu.make_async_copy(
            source, out_refs[side].at[:, columns], out_sems.at[side * peers + mask]
        )
        copy.start()
        stores.append(copy)

    for mask in range(peers):
        store(2, mask)
    sums = sums_refs[0][...]
    for mask in range(1, peers):
        sums = sums + sums_refs[mask][...]
    means = sums[0:2] / width
    for side in range(2):
        scale = scales_ref[side]
        drop = scale * down_rows(means[side : side + 1, :])
        for mask in range(peers):
            columns = head_columns(device ^ mask)
            gain = gains_ref[side : side + 1, columns]
            unit_grad = grads_refs[mask][side].astype(jnp.float32) * gain
            centered = unit_grad - raw_refs[mask][side].astype(jnp.float32) * drop
            outs[side, mask] = (scale * centered).astype(jnp.bfloat16)
            store(side, mask)
            gain_out_refs[side][:, columns] = sums_refs[mask][2 + side : 3 + side, :HD] / gain
    for copy in stores:
        copy.wait()


def swap(array, axis, size, mask):
    return lax.ppermute(array, axis, [(index, index ^ mask) for index in range(size)])


def tp_parts(array, size):
    array = array + swap(array, "tp", size, 1)
    return [array] + [swap(array, "tp", size, mask) for mask in range(2, size, 2)]


def tp_halves(array, size):
    mask = 1
    while mask < size // 2:
        array = array + swap(array, "tp", size, mask)
        mask *= 2
    return [array, swap(array, "tp", size, mask)]


def to_peers(arrays, peers):
    return [arrays[0]] + [swap(arrays[mask], "ctx", peers, mask) for mask in range(1, peers)]


def in_hbm(array):
    return pltpu.with_memory_space_constraint(array, pltpu.HBM)


def call(kernel, out_shape, operands, in_specs, out_specs, scratch_shapes, vmem_mib):
    return pl.pallas_call(
        kernel,
        out_shape=out_shape,
        in_specs=in_specs,
        out_specs=out_specs,
        scratch_shapes=scratch_shapes,
        compiler_params=pltpu.CompilerParams(vmem_limit_bytes=vmem_mib << 20),
    )(*operands)


def whole_heads(peers, tp_size, query_proj, key_proj, value_proj, query_gain, key_gain, stripe_of, grad_out):
    token_count, local_width = query_proj.shape
    width = local_width * tp_size
    rows = token_count * peers
    members = tp_size // 2
    block = math.gcd(rows // 2, 256)
    count = rows // block
    tiles = count * (count + 1) // 2
    shape, semaphores = jax.ShapeDtypeStruct, pltpu.SemaphoreType.DMA
    head = lambda parts: shape((parts, token_count, HD), jnp.bfloat16)
    *blocks, squares, gains, numbers = call(
        functools.partial(cut_kernel, peers),
        [head(2)] * (2 * peers)
        + [
            shape((2, token_count), jnp.float32),
            shape((2, local_width), jnp.float32),
            shape((1, stripe_of.shape[0]), jnp.int32),
        ],
        [
            in_hbm(array)
            for array in (query_proj, key_proj, value_proj, grad_out, query_gain[None], key_gain[None], stripe_of[None])
        ],
        [HBM] * 7,
        [VMEM] * (2 * peers + 3),
        [semaphores((4 * peers + 3,))],
        8,
    )
    raw, plain = blocks[:peers], to_peers(blocks[peers:], peers)
    half = shape((2, token_count // 2, HD), jnp.bfloat16)
    *normed, scales = call(
        functools.partial(normalize_kernel, peers, width, members),
        [half] * (2 * peers) + [shape((2, token_count, HD), jnp.float32)],
        (numbers, gains, *tp_parts(squares, tp_size), *raw),
        [VMEM] + [VMEM] * (1 + members + peers),
        [VMEM] * (2 * peers + 1),
        [],
        8,
    )
    low_normed = to_peers(normed[:peers], peers)
    high_normed = to_peers(normed[peers:], peers)
    whole_head = shape((rows, HD), jnp.bfloat16)
    grad, grad_probs = call(
        functools.partial(grad_probs_kernel, peers, block),
        [whole_head, shape((tiles * block, block), jnp.float32)],
        (numbers, *plain),
        [VMEM] + [VMEM] * peers,
        [VMEM] * 2,
        [pltpu.VMEM((rows, HD), jnp.bfloat16)],
        8,
    )
    low = rows // 2
    low_head = lambda dtype: shape((low, HD), dtype)
    scratch = lambda keys, queries: [
        pltpu.VMEM((2, keys, block), jnp.float32),
        pltpu.VMEM((keys, queries), jnp.bfloat16),
        pltpu.VMEM((keys, queries), jnp.bfloat16),
    ]
    low_results = call(
        functools.partial(low_kernel, peers, block),
        [low_head(jnp.bfloat16)] * 3
        + [low_head(jnp.float32)] * 2
        + [shape((peers, token_count // 2), jnp.float32), shape((1, HD), jnp.float32)],
        (numbers, grad, grad_probs, *low_normed),
        [VMEM] + [VMEM] * (2 + peers),
        [VMEM] * 7,
        [pltpu.VMEM((low, HD), jnp.float32)] + scratch(low, low),
        16,
    )
    *grads, sums, gain_sums = call(
        functools.partial(high_kernel, peers, block),
        [head(3)] * peers + [shape((2 * peers, token_count), jnp.float32), shape((2, HD), jnp.float32)],
        (numbers, grad, grad_probs, *high_normed, *low_results),
        [VMEM] + [VMEM] * (2 + peers + 7),
        [VMEM] * (peers + 2),
        [
            pltpu.VMEM((low, HD), jnp.bfloat16),
            pltpu.VMEM((rows, HD), jnp.bfloat16),
            pltpu.VMEM((low, HD), jnp.float32),
            pltpu.VMEM((rows, HD), jnp.float32),
            pltpu.VMEM((rows, HD), jnp.bfloat16),
        ]
        + scratch(rows, low),
        24,
    )
    grads = to_peers(grads, peers)
    totals = call(
        functools.partial(totals_kernel, peers, 2),
        [shape((4, token_count), jnp.float32)] * peers,
        (gain_sums, *tp_halves(sums, tp_size)),
        [VMEM] * 3,
        [VMEM] * peers,
        [],
        8,
    )
    totals = to_peers(totals, peers)
    whole_out = shape((token_count, local_width), jnp.bfloat16)
    row = shape((1, local_width), jnp.float32)
    grad_query, grad_key, grad_value, query_gain_grad, key_gain_grad = call(
        functools.partial(finish_kernel, peers, width),
        [whole_out] * 3 + [row] * 2,
        (scales, gains, *raw, *grads, *totals),
        [VMEM] * (2 + 3 * peers),
        [ANY] * 3 + [VMEM] * 2,
        [
            pltpu.VMEM((2, peers, token_count, HD), jnp.bfloat16),
            semaphores((3 * peers,)),
        ],
        8,
    )
    return (grad_query, grad_key, grad_value, query_gain_grad[0], key_gain_grad[0])


def row_positions(stripe_list, offset, count, stripe):
    storage_rows = offset + lax.iota(jnp.int32, count)
    stripe_ids = lax.iota(jnp.int32, stripe_list.shape[0])
    matches = (storage_rows // stripe)[:, None] == stripe_ids[None, :]
    chosen = jnp.sum(jnp.where(matches, stripe_list[None, :], 0), axis=1)
    return chosen * stripe + storage_rows % stripe


def block_scores(query_heads, grad_heads, query_places, key_heads, value_heads, key_places):
    scores = jnp.einsum(
        "thd,khd->htk", query_heads, key_heads, preferred_element_type=jnp.float32
    ) * HD ** (-0.5)
    visible = key_places[None, :] <= query_places[:, None]
    scores = jnp.where(visible[None], scores, -jnp.inf)
    grad_probs = jnp.einsum(
        "thd,khd->htk", grad_heads, value_heads, preferred_element_type=jnp.float32
    )
    return (scores, grad_probs)


def block_weights(scores, grad_probs, log_total, row_delta):
    probs = jnp.exp(scores - log_total[:, :, None])
    grad_scores = probs * (grad_probs - row_delta[:, :, None])
    return (probs.astype(jnp.bfloat16), grad_scores.astype(jnp.bfloat16))


def finish_norm(inverse_norm, unit_rows, unit_grad, mean_rows):
    return (inverse_norm * (unit_grad - unit_rows * mean_rows[:, None])).astype(jnp.bfloat16)


def gathered_blocks(tp_size, query_proj, key_proj, value_proj, query_gain, key_gain, stripe_of, grad_out):
    token_count, local_width = query_proj.shape
    local_heads = local_width // HD
    width = local_width * tp_size
    stripe = token_count // 2
    device = lax.axis_index("ctx")
    query_rows = query_proj.astype(jnp.float32)
    key_rows = key_proj.astype(jnp.float32)
    query_square, key_square = lax.psum(
        (jnp.sum(query_rows * query_rows, axis=1), jnp.sum(key_rows * key_rows, axis=1)), "tp"
    )
    query_inverse = lax.rsqrt(query_square / width + EPSILON)[:, None]
    key_inverse = lax.rsqrt(key_square / width + EPSILON)[:, None]
    query_unit = query_rows * query_inverse
    key_unit = key_rows * key_inverse
    query_normed = (query_unit * query_gain).astype(jnp.bfloat16)
    key_normed = (key_unit * key_gain).astype(jnp.bfloat16)
    query_places = row_positions(stripe_of, device * token_count, token_count, stripe)
    query_heads = query_normed.reshape(token_count, local_heads, HD)
    grad_heads = grad_out.reshape(token_count, local_heads, HD)
    key_heads = key_normed.reshape(token_count, local_heads, HD)
    value_heads = value_proj.reshape(token_count, local_heads, HD)
    start_best = jnp.full((local_heads, token_count), -1e30, jnp.float32)
    zero_rows = jnp.zeros((local_heads, token_count), jnp.float32)
    key_piece = lax.all_gather(key_normed, "ctx", axis=0, tiled=True)
    value_piece = lax.all_gather(value_proj, "ctx", axis=0, tiled=True)
    row_count = key_piece.shape[0]
    block = math.gcd(row_count, 512)
    key_blocks = key_piece.reshape(row_count // block, block, local_heads, HD)
    value_blocks = value_piece.reshape(row_count // block, block, local_heads, HD)

    def forward_advance(status, entry):
        row_best, row_total, weighted = status
        key_block, value_block, block_index = entry
        key_places = row_positions(stripe_of, block_index * block, block, stripe)
        scores, grad_probs = block_scores(
            query_heads, grad_heads, query_places, key_block, value_block, key_places
        )
        new_best = jnp.maximum(row_best, jnp.max(scores, axis=2))
        decay_factor = jnp.exp(row_best - new_best)
        exponent = jnp.exp(scores - new_best[:, :, None])
        return (
            (
                new_best,
                row_total * decay_factor + jnp.sum(exponent, axis=2),
                weighted * decay_factor + jnp.sum(exponent * grad_probs, axis=2),
            ),
            None,
        )

    block_ids = jnp.arange(row_count // block, dtype=jnp.int32)
    row_best, row_total, weighted = lax.scan(
        forward_advance, (start_best, zero_rows, zero_rows), (key_blocks, value_blocks, block_ids)
    )[0]
    log_total = row_best + jnp.log(row_total)
    row_delta = weighted / row_total
    zero_grads = jnp.zeros((token_count, local_heads, HD), jnp.float32)
    total_all, delta_all = (
        lax.all_gather(log_total, "ctx", axis=1, tiled=True),
        lax.all_gather(row_delta, "ctx", axis=1, tiled=True),
    )

    def query_fold(carry_state, pieces):
        query_piece, grad_piece = pieces
        row_count = query_piece.shape[0]
        block = math.gcd(row_count, 512)
        query_blocks = query_piece.reshape(row_count // block, block, local_heads, HD)
        grad_blocks = grad_piece.reshape(row_count // block, block, local_heads, HD)

        def query_advance(status, entry):
            key_grad, value_grad = status
            query_block, grad_block, block_index = entry
            first_row = block_index * block
            block_places = row_positions(stripe_of, first_row, block, stripe)
            block_total = lax.dynamic_slice_in_dim(total_all, first_row, block, 1)
            block_delta = lax.dynamic_slice_in_dim(delta_all, first_row, block, 1)
            scores, grad_probs = block_scores(
                query_block, grad_block, block_places, key_heads, value_heads, query_places
            )
            probs_rounded, scores_rounded = block_weights(
                scores, grad_probs, block_total, block_delta
            )
            value_grad = value_grad + jnp.einsum(
                "htk,thd->khd", probs_rounded, grad_block, preferred_element_type=jnp.float32
            )
            key_grad = key_grad + jnp.einsum(
                "htk,thd->khd", scores_rounded, query_block, preferred_element_type=jnp.float32
            )
            return ((key_grad, value_grad), None)

        block_ids = jnp.arange(row_count // block, dtype=jnp.int32)
        return lax.scan(query_advance, carry_state, (query_blocks, grad_blocks, block_ids))[0]

    key_grad, value_grad = query_fold(
        (zero_grads, zero_grads),
        (
            lax.all_gather(query_normed, "ctx", axis=0, tiled=True),
            lax.all_gather(grad_out, "ctx", axis=0, tiled=True),
        ),
    )

    def key_fold(carry_state, pieces):
        key_piece, value_piece = pieces
        row_count = key_piece.shape[0]
        block = math.gcd(row_count, 512)
        key_blocks = key_piece.reshape(row_count // block, block, local_heads, HD)
        value_blocks = value_piece.reshape(row_count // block, block, local_heads, HD)

        def key_advance(query_grad, entry):
            key_block, value_block, block_index = entry
            key_places = row_positions(stripe_of, block_index * block, block, stripe)
            scores, grad_probs = block_scores(
                query_heads, grad_heads, query_places, key_block, value_block, key_places
            )
            _, scores_rounded = block_weights(scores, grad_probs, log_total, row_delta)
            query_grad = query_grad + jnp.einsum(
                "htk,khd->thd", scores_rounded, key_block, preferred_element_type=jnp.float32
            )
            return (query_grad, None)

        block_ids = jnp.arange(row_count // block, dtype=jnp.int32)
        return lax.scan(key_advance, carry_state, (key_blocks, value_blocks, block_ids))[0]

    query_grad = key_fold(
        zero_grads,
        (
            lax.all_gather(key_normed, "ctx", axis=0, tiled=True),
            lax.all_gather(value_proj, "ctx", axis=0, tiled=True),
        ),
    )
    inverse_root = HD ** (-0.5)
    query_normed_grad = (query_grad * inverse_root).reshape(token_count, local_width)
    key_normed_grad = (key_grad * inverse_root).reshape(token_count, local_width)
    grad_value = value_grad.reshape(token_count, local_width).astype(jnp.bfloat16)
    query_unit_grad = query_normed_grad * query_gain
    key_unit_grad = key_normed_grad * key_gain
    query_mean_terms, key_mean_terms = lax.psum(
        (jnp.sum(query_unit_grad * query_unit, axis=1), jnp.sum(key_unit_grad * key_unit, axis=1)),
        "tp",
    )
    grad_query = finish_norm(query_inverse, query_unit, query_unit_grad, query_mean_terms / width)
    grad_key = finish_norm(key_inverse, key_unit, key_unit_grad, key_mean_terms / width)
    grad_query_gain, grad_key_gain = lax.psum(
        (
            jnp.sum(query_normed_grad * query_unit, axis=0),
            jnp.sum(key_normed_grad * key_unit, axis=0),
        ),
        "ctx",
    )
    return (grad_query, grad_key, grad_value, grad_query_gain, grad_key_gain)


def solution(mesh):
    peers, tp_size = mesh.shape["ctx"], mesh.shape["tp"]

    def per_device(query_proj, *others):
        local_heads = query_proj.shape[1] // HD
        whole = local_heads == peers and peers & (peers - 1) == 0 and tp_size & (tp_size - 1) == 0
        if not whole:
            return gathered_blocks(tp_size, query_proj, *others)
        return whole_heads(peers, tp_size, query_proj, *others)

    placed = (P("ctx", "tp"), P("ctx", "tp"), P("ctx", "tp"), P("tp"), P("tp"), P(), P("ctx", "tp"))
    return jax.shard_map(
        per_device,
        mesh=mesh,
        in_specs=placed,
        out_specs=(P("ctx", "tp"), P("ctx", "tp"), P("ctx", "tp"), P("tp"), P("tp")),
        check_vma=False,
    )
```
